256 devices in a mesh: tm: 64 (over z, x, core), head: 4 (over y).
Axes of the slice: x: 4, y: 4, z: 8, core: 2. Of those that a mesh axis runs over, the one named last changes fastest.
Arguments:
- frames: bfloat16 [65536, 1024], P('tm'), may hold values from -6 to 6
- grad_out: bfloat16 [65536, 1024], P('tm', 'head'), may hold values from -6 to 6
- w_query: bfloat16 [1024, 1024], P(None, 'head'), may hold values from -0.1875 to 0.1875
- w_key: bfloat16 [1024, 1024], P(None, 'head'), may hold values from -0.1875 to 0.1875
- w_value: bfloat16 [1024, 1024], P(None, 'head'), may hold values from -0.1875 to 0.1875
Outputs:
- grad_input: bfloat16 [65536, 1024], P('tm', 'head')
- grad_wq: float32 [1024, 1024], P('tm', 'head')
- grad_wk: float32 [1024, 1024], P('tm', 'head')
- grad_wv: float32 [1024, 1024], P('tm', 'head')
The draws below stay inside these ranges and needn't reach their ends.
All inputs are finite; a program needn't handle non-finite values.
Results may differ from the reference program's by a relative error of at most 0.0095.
Values may be sent and summed in bfloat16 or wider, within the bound.
A program may use at most 64 MiB of HBM per device.

```python
import jax
import jax.numpy as jnp
from jax import lax

D = 1024
H = 16
DH = 64
TOK_DEV = 1024
TOKENS = 65536
HD = 1024
N_HEAD = 4


def levels(key, shape, cuts, smallest, largest):
    gain = 1.0
    for axis_at, blocks in cuts:
        heights = jax.random.uniform(jax.random.fold_in(jax.random.fold_in(key, 6), axis_at), (blocks,), jnp.float32, smallest / len(cuts), largest / len(cuts))
        gain = gain * jnp.repeat(jnp.exp(heights), shape[axis_at] // blocks).reshape((-1,) + (1,) * (len(shape) - 1 - axis_at))
    return gain


def normal_values(stream_key, extent, width, most, pieces=(), kind=jnp.bfloat16):
    values = jax.random.normal(stream_key, extent, jnp.float32) * width
    if len(pieces) > 0:
        values = levels(stream_key, extent, pieces, -0.22, 0.18) * values
    return jnp.clip(values, min=-most, max=most).astype(kind)


def setup_inputs(seed: int = 0) -> dict:
    key_list = jax.random.split(jax.random.key(seed), 6)
    return {
        "frames": normal_values(key_list[0], (TOKENS, D), 1.0, 6.0, ((0, 64),)),
        "grad_out": normal_values(key_list[1], (TOKENS, HD), 1.0, 6.0, ((0, 64), (1, 4))),
        "w_query": normal_values(key_list[2], (D, HD), D ** -0.5, 0.1875, ((1, 4),)),
        "w_key": normal_values(key_list[3], (D, HD), D ** -0.5, 0.1875, ((1, 4),)),
        "w_value": normal_values(key_list[4], (D, HD), D ** -0.5, 0.1875, ((1, 4),)),
    }


def block_grads(items, scale_factor):
    query_rows, key_rows, value_rows, grad_rows, prefix_state, suffix_state = items
    query32 = query_rows.astype(jnp.float32)
    key32 = key_rows.astype(jnp.float32)
    value32 = value_rows.astype(jnp.float32)
    grad32 = grad_rows.astype(jnp.float32)
    causal = jnp.arange(TOK_DEV)[:, None] >= jnp.arange(TOK_DEV)[None, :]
    grad_scores = jnp.einsum('thd,shd->hts', grad32, value32)
    grad_scores = jnp.where(causal[None], grad_scores, 0.0).astype(jnp.bfloat16)
    grad_scores = lax.optimization_barrier(grad_scores).astype(jnp.float32)
    key_scores = jnp.einsum('thd,shd->hts', query32, key32)
    key_scores = jnp.where(causal[None], key_scores, 0.0).astype(jnp.bfloat16)
    key_scores = lax.optimization_barrier(key_scores).astype(jnp.float32)
    query_grad = jnp.einsum('hts,shd->thd', grad_scores, key32) + jnp.einsum(
        'thj,hij->thi', grad32, prefix_state, precision=lax.Precision.HIGHEST)
    key_grad = jnp.einsum('hts,thd->shd', grad_scores, query32) + jnp.einsum(
        'shj,hij->shi', value32, suffix_state, precision=lax.Precision.HIGHEST)
    value_grad = jnp.einsum('hts,thd->shd', key_scores, grad32) + jnp.einsum(
        'shi,hij->shj', key32, suffix_state, precision=lax.Precision.HIGHEST)
    return ((query_grad * scale_factor).astype(jnp.bfloat16),
            (key_grad * scale_factor).astype(jnp.bfloat16),
            (value_grad * scale_factor).astype(jnp.bfloat16))


def reference(frames, grad_out, w_query, w_key, w_value):
    blocks = TOKENS // TOK_DEV
    scale_factor = float(DH * TOKENS) ** -0.5
    query = jnp.dot(frames, w_query, preferred_element_type=jnp.float32).astype(jnp.bfloat16)
    key = jnp.dot(frames, w_key, preferred_element_type=jnp.float32).astype(jnp.bfloat16)
    value = jnp.dot(frames, w_value, preferred_element_type=jnp.float32).astype(jnp.bfloat16)

    def split_heads(array):
        return array.reshape(blocks, TOK_DEV, H, DH)

    query4 = split_heads(query)
    key4 = split_heads(key)
    value4 = split_heads(value)
    grad4 = split_heads(grad_out)
    key_value = jnp.einsum('bthi,bthj->bhij', key4.astype(jnp.float32), value4.astype(jnp.float32),
                           precision=lax.Precision.HIGHEST)
    query_grad = jnp.einsum('bthi,bthj->bhij', query4.astype(jnp.float32), grad4.astype(jnp.float32),
                            precision=lax.Precision.HIGHEST)
    prefix = jnp.cumsum(key_value, axis=0) - key_value
    suffix = jnp.cumsum(query_grad[::-1], axis=0)[::-1] - query_grad
    dquery, dkey, dvalue = lax.map(lambda items: block_grads(items, scale_factor),
                                   (query4, key4, value4, grad4, prefix, suffix))
    dquery = dquery.reshape(TOKENS, HD)
    dkey = dkey.reshape(TOKENS, HD)
    dvalue = dvalue.reshape(TOKENS, HD)
    group_width = HD // N_HEAD
    total = jnp.zeros((TOKENS, D), jnp.float32)
    for group in range(N_HEAD):
        low = group * group_width
        high = low + group_width
        part = jnp.dot(dquery[:, low:high], w_query[:, low:high].T, preferred_element_type=jnp.float32)
        part = part + jnp.dot(dkey[:, low:high], w_key[:, low:high].T, preferred_element_type=jnp.float32)
        part = part + jnp.dot(dvalue[:, low:high], w_value[:, low:high].T, preferred_element_type=jnp.float32)
        rounded = lax.optimization_barrier(part.astype(jnp.bfloat16))
        total = total + rounded.astype(jnp.float32)
    grad_input = total.astype(jnp.bfloat16)
    grad_wq = jnp.dot(frames.T, dquery, preferred_element_type=jnp.float32)
    grad_wk = jnp.dot(frames.T, dkey, preferred_element_type=jnp.float32)
    grad_wv = jnp.dot(frames.T, dvalue, preferred_element_type=jnp.float32)
    return (grad_input, grad_wq, grad_wk, grad_wv)
```

```python
import functools

import jax
import jax.numpy as jnp
from jax import lax
from jax.experimental import pallas as pl
from jax.experimental.pallas import tpu as pltpu
from jax.sharding import PartitionSpec as P

DH = 64
CHUNK = 256
NX = 4
NC = 2
MESH = pl.DeviceIdType.MESH
BF = jnp.bfloat16
F32 = jnp.float32


def nn(a, b):
    return lax.dot_general(a, b, (((1,), (0,)), ((), ())), preferred_element_type=F32)


def nt(a, b):
    return lax.dot_general(a, b, (((1,), (1,)), ((), ())), preferred_element_type=F32)


def tn(a, b):
    return lax.dot_general(a, b, (((0,), (0,)), ((), ())), preferred_element_type=F32)


def split(value):
    high = value.astype(BF)
    return high, (value - high.astype(F32)).astype(BF)


def kernel(
    dims,
    frames_hbm, grad_hbm, wq_hbm, wk_hbm, wv_hbm,
    gi_ref, gwq_ref, gwk_ref, gwv_ref,
    fr, g_tok, w_all, q_tok, qt, kt, vt, gt, frt,
    kvc, qgc, st, stb, sc_r1, sc_k, sc_zr, sc_acc, sc_p, sc_xr, sc_e, sc_r4, fin,
    d_in, d_t, parts, y_r1, y_r2,
    wg, c_r, w_s1, x_r1, x_r2, w_s2, w_s2f, z_r,
    in_sem, sc_s, sc_rs, zs_s, zs_r, xs_s, xs_r,
    y_s, y_r, c_s, c_rs, w_s, w_r, wz_s, wz_r,
):
    T, D, G, C, NZ, NY, NH, dh = (
        dims[k] for k in ("T", "D", "G", "C", "NZ", "NY", "NH", "DH")
    )
    NCH = T // C
    NM = NZ * NX * NC
    scale = float(dh * T * NM) ** (-0.5)
    R = D // NM
    DB = D // NY

    me = lax.axis_index("tm")
    y = lax.axis_index("head")
    c = lax.rem(me, NC)
    x = lax.rem(lax.div(me, NC), NX)
    z = lax.div(me, NC * NX)

    def at(zz, xx, cc, yy=None):
        return (zz * (NX * NC) + xx * NC + cc, y if yy is None else yy)

    sib = at(z, x, 1 - c)

    copies_in = [
        pltpu.make_async_copy(
            frames_hbm.at[pl.ds(i * C, C), :], fr.at[pl.ds(i * C, C), :], in_sem.at[4 + i]
        )
        for i in range(NCH)
    ]
    copies_w = [
        pltpu.make_async_copy(ref, w_all.at[:, pl.ds(i * G, G)], in_sem.at[i])
        for i, ref in enumerate((wq_hbm, wk_hbm, wv_hbm))
    ]
    copy_g = pltpu.make_async_copy(grad_hbm, g_tok, in_sem.at[3])
    copies_w[1].start()
    copies_in[0].start()
    copies_w[2].start()
    copies_w[0].start()
    copy_g.start()
    for i in range(1, NCH):
        copies_in[i].start()

    barrier = pltpu.get_barrier_semaphore()
    peers = [sib]
    peers += [at(lax.rem(z + d, NZ), x, c) for d in range(1, NZ)]
    peers += [at(z, lax.rem(x + d, NX), c) for d in range(1, NX)]
    y_next, y_prev, y_far = (lax.rem(y + d, NY) for d in (1, NY - 1, 2))
    peers += [(me, y_next), (me, y_prev)]
    for peer in peers:
        pl.semaphore_signal(barrier, inc=1, device_id=peer, device_id_type=MESH)

    row = lax.broadcasted_iota(jnp.int32, (G, G), 0)
    col = lax.broadcasted_iota(jnp.int32, (G, G), 1)
    same = lax.div(row, dh) == lax.div(col, dh)

    def spread(packed):
        return jnp.where(same, jnp.concatenate([packed] * NH, axis=0), 0.0)

    def pack(full):
        total = full[0:dh]
        for h in range(1, NH):
            total = total + full[h * dh : (h + 1) * dh]
        return total

    copies_w[0].wait()
    copies_w[1].wait()
    copies_w[2].wait()
    copy_g.wait()
    for i in range(NCH):
        copies_in[i].wait()

    def project(i, carry):
        here = pl.ds(pl.multiple_of(i * C, C), C)
        f = fr[here, :]
        k = nn(f, w_all[:, G : 2 * G]).astype(BF).T
        v = nn(f, w_all[:, 2 * G :]).astype(BF).T
        kt[:, here] = k
        vt[:, here] = v
        kvc[i] = jnp.where(same, nt(k, v), 0.0)
        q = nn(f, w_all[:, :G]).astype(BF)
        q_tok[here, :] = q
        qf = q.T
        qt[:, here] = qf
        g = g_tok[here, :]
        gt[:, here] = g.T
        qgc[i] = jnp.where(same, nn(qf, g), 0.0)
        return carry

    lax.fori_loop(0, NCH, project, 0)

    st[0] = pack(sum(kvc[i] for i in range(NCH)))
    st[1] = pack(sum(qgc[i] for i in range(NCH)))
    stb[...] = st[...].astype(BF)
    pl.semaphore_wait(barrier, len(peers))

    def remote(src, dst, send, recv, dev):
        return pltpu.make_async_remote_copy(
            src_ref=src, dst_ref=dst, send_sem=send, recv_sem=recv,
            device_id=dev, device_id_type=MESH,
        )

    scan1 = remote(stb.at[1 - c], sc_r1, sc_s.at[0], sc_rs.at[0], sib)
    scan1.start()

    side = 1 - 2 * c
    zp = z + c * (NZ - 1 - 2 * z)
    xp = x + c * (NX - 1 - 2 * x)

    def z_copy(d):
        return remote(
            sc_k, sc_zr.at[d - 1], zs_s.at[d - 1], zs_r.at[d - 1],
            at(lax.rem(z + side * d + NZ, NZ), x, c),
        )

    def scan_z_start():
        scan1.wait()
        sc_k[...] = (st[c] + sc_r1[...].astype(F32)).astype(BF)
        for d in range(1, NZ):
            @pl.when(zp + d < NZ)
            def _():
                z_copy(d).start()

    def x_copy(d, src):
        return remote(
            src, sc_xr.at[d - 1], xs_s.at[d - 1], xs_r.at[d - 1],
            at(z, lax.rem(x + d, NX), c),
        )

    def scan_x_start():
        sc_acc[...] = jnp.zeros_like(sc_acc)
        for d in range(1, NZ):
            @pl.when(zp + d < NZ)
            def _():
                z_copy(d).wait_send()

            @pl.when(zp >= d)
            def _():
                z_copy(d).wait_recv()
                sc_acc[...] += sc_zr[d - 1].astype(F32)
        own = sc_acc[...]
        sc_p[0] = own.astype(BF)
        sc_p[1] = (own + st[c] + sc_r1[...].astype(F32)).astype(BF)
        for d in range(1, NX):
            xt = lax.rem(x + d, NX)
            later = jnp.where(side * (xt - x) > 0, 1, 0)
            x_copy(d, sc_p.at[later]).start()

    scan4 = remote(sc_e, sc_r4, sc_s.at[1], sc_rs.at[1], sib)

    def scan_core_start():
        for d in range(1, NX):
            xt = lax.rem(x + d, NX)
            later = jnp.where(side * (xt - x) > 0, 1, 0)
            x_copy(d, sc_p.at[later]).wait()
        own = sc_acc[...]
        for d in range(1, NX):
            own = own + sc_xr[d - 1].astype(F32)
        fin[c] = own
        sc_e[...] = (own + st[c]).astype(BF)
        scan4.start()

    def scan_end():
        scan4.wait()
        fin[1 - c] = sc_r4[...].astype(F32)

    tri = lax.broadcasted_iota(jnp.int32, (C, C), 0) >= lax.broadcasted_iota(
        jnp.int32, (C, C), 1
    )
    lane_head = lax.div(lax.broadcasted_iota(jnp.int32, (C, G), 1), dh)

    def intra(i):
        here = pl.ds(i * C, C)
        g = g_tok[here, :]
        q = q_tok[here, :]
        kf, vf, qf, gf = kt[:, here], vt[:, here], qt[:, here], gt[:, here]
        zero = jnp.zeros_like(g)
        for h in range(NH):
            rows = slice(h * dh, (h + 1) * dh)
            pg = nn(jnp.where(lane_head == h, g, zero), vf)
            pg = jnp.where(tri, pg, 0.0).astype(BF)
            sk = nn(jnp.where(lane_head == h, q, zero), kf)
            sk = jnp.where(tri, sk, 0.0).astype(BF)
            d_in[pl.ds(h * dh, dh), here] = nt(kf[rows], pg)
            d_in[pl.ds(G + h * dh, dh), here] = nn(qf[rows], pg)
            d_in[pl.ds(2 * G + h * dh, dh), here] = nn(gf[rows], sk)

    def flip(i):
        here = pl.ds(i * C, C)
        for b in range(D // C):
            frt[pl.ds(b * C, C), here] = fr[here, pl.ds(b * C, C)].T

    intra(0)
    scan_z_start()
    intra(1)
    flip(0)
    intra(2)
    flip(1)
    scan_x_start()
    intra(3)
    flip(2)
    scan_core_start()
    flip(3)
    scan_end()

    def finish(i):
        here = pl.ds(i * C, C)
        prefix = spread(fin[0])
        suffix = spread(fin[1])
        for j in range(i):
            prefix = prefix + kvc[j]
        for j in range(i + 1, NCH):
            suffix = suffix + qgc[j]
        ph, pe = split(prefix)
        sh, se = split(suffix)
        kf, vf, gf = kt[:, here], vt[:, here], gt[:, here]
        dq = d_in[pl.ds(0, G), here] + nn(ph, gf) + nn(pe, gf)
        dk = d_in[pl.ds(G, G), here] + nn(sh, vf) + nn(se, vf)
        dv = d_in[pl.ds(2 * G, G), here] + tn(sh, kf) + tn(se, kf)
        d_t[pl.ds(0, G), here] = (dq * scale).astype(BF)
        d_t[pl.ds(G, G), here] = (dk * scale).astype(BF)
        d_t[pl.ds(2 * G, G), here] = (dv * scale).astype(BF)

    HB = DB // 2

    def part(i):
        here = pl.ds(i * C, C)
        grads = d_t[:, here]
        for d in (2, 1, NY - 1, 0):
            b = lax.rem(y + d, NY)
            rows = pl.ds(pl.multiple_of(b * DB, DB), DB)
            value = nn(w_all[rows, :], grads).astype(BF)
            parts[i, b] = value.reshape(2, HB, C)
            if d == 2:
                y_copy(i, 0).start()
                y_copy(i, 1).start()
            if d == 1:
                y_copy(i, 2).start()
            if d == NY - 1:
                y_copy(i, 3).start()

    def y_copy(i, n):
        src, dst, dev = (
            (parts.at[i, y_far, 0], y_r1.at[i, 0], y_next),
            (parts.at[i, y_far, 1], y_r1.at[i, 1], y_prev),
            (parts.at[i, y_next, 1], y_r2.at[i, 0, 1], y_next),
            (parts.at[i, y_prev, 0], y_r2.at[i, 1, 0], y_prev),
            (parts.at[i, y_next, 0], y_r2.at[i, 0, 0], y_next),
            (parts.at[i, y_prev, 1], y_r2.at[i, 1, 1], y_prev),
        )[n]
        return remote(src, dst, y_s.at[i, n], y_r.at[i, n], (me, dev))

    def y_relay(i):
        for n, dest, half in ((0, y_next, 0), (1, y_prev, 1)):
            y_copy(i, n).wait()
            parts[i, dest, half] = (
                parts[i, dest, half].astype(F32) + y_r1[i, half].astype(F32)
            ).astype(BF)
            y_copy(i, 4 + n).start()

    def y_final(i):
        for n in range(2, 6):
            y_copy(i, n).wait()
        total = parts[i, y].astype(F32) + y_r2[i, 0].astype(F32) + y_r2[i, 1].astype(F32)
        gi_ref[pl.ds(i * C, C), :] = total.reshape(DB, C).astype(BF).T

    def c_copy(w):
        return remote(
            wg.at[w, :, :, 1 - c], c_r.at[w], c_s.at[w], c_rs.at[w], sib
        )

    def weight(w):
        cols = d_t[pl.ds(w * G, G), :]

        def block(i, carry):
            rows = pl.ds(pl.multiple_of(i * (D // NZ), D // NZ), D // NZ)
            value = nt(frt[rows, :], cols)
            wg[w, i] = value.astype(BF).reshape(NX, NC, R, G)
            return carry

        lax.fori_loop(0, NZ, block, 0)
        c_copy(w).start()

    x_next, x_prev, x_far = (lax.rem(x + d, NX) for d in (1, NX - 1, 2))

    def xw_copy(w, n):
        src, dst, dev = (
            (w_s1.at[w, x_far, 0], x_r1.at[w, 0], x_next),
            (w_s1.at[w, x_far, 1], x_r1.at[w, 1], x_prev),
            (w_s1.at[w, x_next, 1], x_r2.at[w, 0, 1], x_next),
            (w_s1.at[w, x_prev, 0], x_r2.at[w, 1, 0], x_prev),
            (w_s1.at[w, x_next, 0], x_r2.at[w, 0, 0], x_next),
            (w_s1.at[w, x_prev, 1], x_r2.at[w, 1, 1], x_prev),
        )[n]
        return remote(src, dst, w_s.at[w, n], w_r.at[w, n], at(z, dev, c))

    def w_core(w):
        c_copy(w).wait()
        for b in range(NX):
            value = wg[w, :, b, c].astype(F32) + c_r[w, :, b].astype(F32)
            w_s1[w, b] = value.astype(BF).reshape(2, NZ // 2, R, G)
        for n in range(4):
            xw_copy(w, n).start()

    def w_relay(w):
        for n, dest, half in ((0, x_next, 0), (1, x_prev, 1)):
            xw_copy(w, n).wait()
            w_s1[w, dest, half] = (
                w_s1[w, dest, half].astype(F32) + x_r1[w, half].astype(F32)
            ).astype(BF)
            xw_copy(w, 4 + n).start()

    def wz_copy(w, d):
        zt = lax.rem(z + d, NZ)
        return remote(
            w_s2.at[w, zt], z_r.at[w, d - 1], wz_s.at[w, d - 1], wz_r.at[w, d - 1],
            at(zt, x, c),
        )

    def w_cross(w):
        for n in range(2, 6):
            xw_copy(w, n).wait()
        value = w_s1[w, x].astype(F32) + x_r2[w, 0].astype(F32) + x_r2[w, 1].astype(F32)
        value = value.reshape(NZ, R, G)
        w_s2f[w] = value
        w_s2[w] = value.astype(BF)
        for d in range(1, NZ):
            wz_copy(w, d).start()

    def w_final(w, out):
        total = w_s2f[w, z]
        for d in range(1, NZ):
            wz_copy(w, d).wait()
            total = total + z_r[w, d - 1].astype(F32)
        out[...] = total

    finish(0)
    part(0)
    finish(1)
    part(1)
    y_relay(0)
    finish(2)
    finish(3)
    weight(0)
    weight(1)
    w_core(0)
    part(2)
    y_relay(1)
    weight(2)
    w_core(1)
    w_relay(0)
    part(3)
    y_relay(2)
    w_core(2)
    w_relay(1)
    w_cross(0)
    w_relay(2)
    y_relay(3)
    w_cross(1)
    y_final(0)
    w_cross(2)
    y_final(1)
    w_final(0, gwq_ref)
    w_final(1, gwk_ref)
    w_final(2, gwv_ref)
    y_final(2)
    y_final(3)


def build(mesh, interpret_dims=None):
    chunk, dh = interpret_dims or (CHUNK, DH)

    def local(frames, grad_out, w_query, w_key, w_value):
        T, D = frames.shape
        G = w_query.shape[1]
        NM, NY = mesh.shape["tm"], mesh.shape["head"]
        NZ = NM // (NX * NC)
        NH = G // dh
        C = chunk
        NCH = T // C
        R, DB = D // NM, D // NY
        HB = DB // 2
        dims = dict(T=T, D=D, G=G, C=C, NZ=NZ, NY=NY, NH=NH, DH=dh)
        V = pltpu.VMEM
        S = pltpu.SemaphoreType.DMA
        scratch = [
            V((T, D), BF), V((T, G), BF), V((D, 3 * G), BF), V((T, G), BF),
            V((G, T), BF), V((G, T), BF), V((G, T), BF), V((G, T), BF), V((D, T), BF),
            V((NCH, G, G), F32), V((NCH, G, G), F32),
            V((2, dh, G), F32), V((2, dh, G), BF),
            V((dh, G), BF), V((dh, G), BF), V((NZ - 1, dh, G), BF), V((dh, G), F32),
            V((2, dh, G), BF), V((NX - 1, dh, G), BF), V((dh, G), BF), V((dh, G), BF),
            V((2, dh, G), F32),
            V((3 * G, T), F32), V((3 * G, T), BF),
            V((NCH, NY, 2, HB, C), BF), V((NCH, 2, HB, C), BF), V((NCH, 2, 2, HB, C), BF),
            V((3, NZ, NX, NC, R, G), BF), V((3, NZ, NX, R, G), BF),
            V((3, NX, 2, NZ // 2, R, G), BF), V((3, 2, NZ // 2, R, G), BF),
            V((3, 2, 2, NZ // 2, R, G), BF),
            V((3, NZ, R, G), BF), V((3, NZ, R, G), F32), V((3, NZ - 1, R, G), BF),
            S((4 + NCH,)), S((2,)), S((2,)), S((NZ - 1,)), S((NZ - 1,)), S((NX - 1,)), S((NX - 1,)),
            S((NCH, 6)), S((NCH, 6)), S((3,)), S((3,)), S((3, 6)), S((3, 6)),
            S((3, NZ - 1)), S((3, NZ - 1)),
        ]
        anyspace = pl.BlockSpec(memory_space=pl.ANY)
        vm = pl.BlockSpec(memory_space=pltpu.VMEM)
        return pl.pallas_call(
            functools.partial(kernel, dims),
            out_shape=[
                jax.ShapeDtypeStruct((T, DB), BF),
                jax.ShapeDtypeStruct((R, G), F32),
                jax.ShapeDtypeStruct((R, G), F32),
                jax.ShapeDtypeStruct((R, G), F32),
            ],
            in_specs=[anyspace] * 5,
            out_specs=[vm] * 4,
            scratch_shapes=scratch,
            compiler_params=pltpu.CompilerParams(
                collective_id=0, has_side_effects=True, vmem_limit_bytes=48 * 2**20
            ),
        )(frames, grad_out, w_query, w_key, w_value)

    placed = (P("tm", None), P("tm", "head"), P(None, "head"), P(None, "head"), P(None, "head"))
    return jax.shard_map(
        local,
        mesh=mesh,
        in_specs=placed,
        out_specs=(P("tm", "head"), P("tm", "head"), P("tm", "head"), P("tm", "head")),
        check_vma=False,
    )


def solution(mesh):
    return build(mesh)
```

```python
import functools

import jax
import jax.numpy as jnp
from jax import lax
from jax.experimental import pallas as pl
from jax.experimental.pallas import tpu as pltpu
from jax.sharding import PartitionSpec as P

DH = 64
CHUNK = 256
NX = 4
NC = 2
MESH = pl.DeviceIdType.MESH
BF = jnp.bfloat16
F32 = jnp.float32


def nn(a, b):
    return lax.dot_general(a, b, (((1,), (0,)), ((), ())), preferred_element_type=F32)


def nt(a, b):
    return lax.dot_general(a, b, (((1,), (1,)), ((), ())), preferred_element_type=F32)


def tn(a, b):
    return lax.dot_general(a, b, (((0,), (0,)), ((), ())), preferred_element_type=F32)


def split(value):
    high = value.astype(BF)
    return high, (value - high.astype(F32)).astype(BF)


def kernel(
    dims,
    frames_hbm, grad_hbm, wq_hbm, wk_hbm, wv_hbm,
    gi_ref, gwq_ref, gwk_ref, gwv_ref,
    fr, g_tok, w_all, q_tok, qt, kt, vt, gt, frt,
    kvc, qgc, st, stb, sc_r1, sc_k, sc_zs, sc_zr, sc_acc, sc_p, sc_xr, sc_e, sc_r4, fin,
    d_in, d_t, parts, y_r1, y_r2,
    gi_buf, gw_buf, wg, c_r, w_s1, x_r1, x_r2, w_s2, w_s2f, z_r,
    in_sem, out_sem, sc_s, sc_rs, zs_r, xs_r, y_s, y_r, c_rs, w_s, w_r, wz_r,
):
    T, D, G, C, NZ, NY, NH, dh = (
        dims[k] for k in ("T", "D", "G", "C", "NZ", "NY", "NH", "DH")
    )
    NCH = T // C
    NM = NZ * NX * NC
    scale = float(dh * T * NM) ** (-0.5)
    R = D // NM
    DB = D // NY

    me = lax.axis_index("tm")
    y = lax.axis_index("head")
    c = lax.rem(me, NC)
    x = lax.rem(lax.div(me, NC), NX)
    z = lax.div(me, NC * NX)

    def at(zz, xx, cc, yy=None):
        return (zz * (NX * NC) + xx * NC + cc, y if yy is None else yy)

    sib = at(z, x, 1 - c)

    copies_in = [
        pltpu.make_async_copy(
            frames_hbm.at[pl.ds(i * C, C), :], fr.at[pl.ds(i * C, C), :], in_sem.at[4 + i]
        )
        for i in range(NCH)
    ]
    copies_w = [
        pltpu.make_async_copy(ref, w_all.at[:, pl.ds(i * G, G)], in_sem.at[i])
        for i, ref in enumerate((wq_hbm, wk_hbm, wv_hbm))
    ]
    copy_g = pltpu.make_async_copy(grad_hbm, g_tok, in_sem.at[3])
    copies_in[0].start()
    copies_w[1].start()
    copies_w[2].start()
    copies_w[0].start()
    copy_g.start()
    for i in range(1, NCH):
        copies_in[i].start()

    barrier = pltpu.get_barrier_semaphore()
    peers = [sib]
    peers += [at(lax.rem(z + d, NZ), x, c) for d in range(1, NZ)]
    peers += [at(z, lax.rem(x + d, NX), c) for d in range(1, NX)]
    y_next, y_prev, y_far = (lax.rem(y + d, NY) for d in (1, NY - 1, 2))
    peers += [(me, y_next), (me, y_prev)]
    for peer in peers:
        pl.semaphore_signal(barrier, inc=1, device_id=peer, device_id_type=MESH)

    row = lax.broadcasted_iota(jnp.int32, (G, G), 0)
    col = lax.broadcasted_iota(jnp.int32, (G, G), 1)
    same = lax.div(row, dh) == lax.div(col, dh)

    def spread(packed):
        return jnp.where(same, jnp.concatenate([packed] * NH, axis=0), 0.0)

    def pack(full):
        total = full[0:dh]
        for h in range(1, NH):
            total = total + full[h * dh : (h + 1) * dh]
        return total

    def wait_in():
        for copy in copies_w:
            copy.wait()
        copy_g.wait()

    wait_in()

    def project(i, carry):
        here = pl.ds(pl.multiple_of(i * C, C), C)
        pltpu.make_async_copy(frames_hbm.at[here, :], fr.at[here, :], in_sem.at[4 + i]).wait()
        f = fr[here, :]
        k = nn(f, w_all[:, G : 2 * G]).astype(BF).T
        v = nn(f, w_all[:, 2 * G :]).astype(BF).T
        kt[:, here] = k
        vt[:, here] = v
        kvc[i] = jnp.where(same, nt(k, v), 0.0)
        q = nn(f, w_all[:, :G]).astype(BF)
        q_tok[here, :] = q
        qf = q.T
        qt[:, here] = qf
        g = g_tok[here, :]
        gt[:, here] = g.T
        qgc[i] = jnp.where(same, nn(qf, g), 0.0)
        return carry

    lax.fori_loop(0, NCH, project, 0)

    st[0] = pack(sum(kvc[i] for i in range(NCH)))
    st[1] = pack(sum(qgc[i] for i in range(NCH)))
    stb[...] = st[...].astype(BF)
    pl.semaphore_wait(barrier, len(peers))

    def remote(src, dst, send, recv, dev):
        return pltpu.make_async_remote_copy(
            src_ref=src, dst_ref=dst, send_sem=send, recv_sem=recv,
            device_id=dev, device_id_type=MESH,
        )

    def take(ref, sem):
        pltpu.make_async_copy(ref, ref, sem).wait()

    scan1 = remote(stb.at[1 - c], sc_r1, sc_s.at[0], sc_rs.at[0], sib)
    scan1.start()

    side = 1 - 2 * c
    zp = z + c * (NZ - 1 - 2 * z)
    xp = x + c * (NX - 1 - 2 * x)

    hd = dh // 2
    far_first = sorted(range(1, NZ), key=lambda n: -min(n, NZ - n))

    def z_copy(half, d):
        return remote(
            sc_zs.at[half], sc_zr.at[half, d - 1], sc_s.at[2], zs_r.at[half, d - 1],
            at(lax.rem(z + side * d + NZ, NZ), x, c),
        )

    def z_start(half):
        for d in far_first:
            @pl.when(zp + d < NZ)
            def _():
                z_copy(half, d).start()

    def z_gather(half):
        rows = pl.ds(half * hd, hd)
        for d in range(1, NZ):
            @pl.when(zp >= d)
            def _():
                z_copy(half, d).wait_recv()
                sc_acc[rows] += sc_zr[half, d - 1].astype(F32)

    def x_copy(half, d, src):
        return remote(
            src, sc_xr.at[half, d - 1], sc_s.at[3], xs_r.at[half, d - 1],
            at(z, lax.rem(x + d, NX), c),
        )

    def scan_start():
        scan1.wait_recv()
        chip = st[c] + sc_r1[...].astype(F32)
        sc_k[...] = chip
        sc_p[2] = chip[hd:].astype(BF)
        sc_zs[0] = chip[:hd].astype(BF)
        for d in range(1, NX):
            x_copy(1, d, sc_p.at[2]).start()
        z_start(0)
        sc_acc[...] = jnp.zeros_like(sc_acc)

    def scan_mid_b():
        total = sc_k[pl.ds(hd, hd)]
        ahead = jnp.zeros_like(total)
        for d in range(1, NX):
            x_copy(1, d, sc_p.at[2]).wait_recv()
        for d in range(1, NX):
            xs = lax.rem(x + NX - d, NX)
            value = sc_xr[1, d - 1].astype(F32)
            total = total + value
            ahead = ahead + jnp.where(side * (x - xs) > 0, value, 0.0)
        sc_acc[pl.ds(hd, hd)] = ahead
        sc_zs[1] = total.astype(BF)
        z_start(1)

    def scan_mid_a():
        z_gather(0)
        own = sc_acc[pl.ds(0, hd)]
        sc_p[0] = own.astype(BF)
        sc_p[1] = (own + sc_k[pl.ds(0, hd)]).astype(BF)
        for d in range(1, NX):
            xt = lax.rem(x + d, NX)
            later = jnp.where(side * (xt - x) > 0, 1, 0)
            x_copy(0, d, sc_p.at[later]).start()

    def scan_fin():
        for d in range(1, NX):
            x_copy(0, d, sc_p.at[0]).wait_recv()
        own = sc_acc[pl.ds(0, hd)]
        for d in range(1, NX):
            own = own + sc_xr[0, d - 1].astype(F32)
        sc_acc[pl.ds(0, hd)] = own
        z_gather(1)
        own = sc_acc[...]
        fin[c] = own
        sc_e[...] = (own + st[c]).astype(BF)
        scan4.start()

    scan4 = remote(sc_e, sc_r4, sc_s.at[1], sc_rs.at[1], sib)

    def scan_end():
        scan4.wait_recv()
        fin[1 - c] = sc_r4[...].astype(F32)

    tri = lax.broadcasted_iota(jnp.int32, (C, C), 0) >= lax.broadcasted_iota(
        jnp.int32, (C, C), 1
    )
    lane_head = lax.div(lax.broadcasted_iota(jnp.int32, (C, G), 1), dh)

    def intra(i):
        here = pl.ds(i * C, C)
        g = g_tok[here, :]
        q = q_tok[here, :]
        kf, vf, qf, gf = kt[:, here], vt[:, here], qt[:, here], gt[:, here]
        zero = jnp.zeros_like(g)
        for h in range(NH):
            rows = slice(h * dh, (h + 1) * dh)
            pg = nn(jnp.where(lane_head == h, g, zero), vf)
            pg = jnp.where(tri, pg, 0.0).astype(BF)
            sk = nn(jnp.where(lane_head == h, q, zero), kf)
            sk = jnp.where(tri, sk, 0.0).astype(BF)
            d_in[pl.ds(h * dh, dh), here] = nt(kf[rows], pg)
            d_in[pl.ds(G + h * dh, dh), here] = nn(qf[rows], pg)
            d_in[pl.ds(2 * G + h * dh, dh), here] = nn(gf[rows], sk)

    def flip(i):
        here = pl.ds(i * C, C)
        for b in range(D // C):
            frt[pl.ds(b * C, C), here] = fr[here, pl.ds(b * C, C)].T

    intra(0)
    scan_start()
    intra(1)
    flip(0)
    flip(1)
    intra(2)
    scan_mid_b()
    intra(3)
    flip(2)
    flip(3)
    scan_mid_a()
    scan_fin()
    scan_end()

    def finish(i):
        here = pl.ds(i * C, C)
        prefix = spread(fin[0])
        suffix = spread(fin[1])
        for j in range(i):
            prefix = prefix + kvc[j]
        for j in range(i + 1, NCH):
            suffix = suffix + qgc[j]
        ph, pe = split(prefix)
        sh, se = split(suffix)
        kf, vf, gf = kt[:, here], vt[:, here], gt[:, here]
        dq = d_in[pl.ds(0, G), here] + nn(ph, gf) + nn(pe, gf)
        dk = d_in[pl.ds(G, G), here] + nn(sh, vf) + nn(se, vf)
        dv = d_in[pl.ds(2 * G, G), here] + tn(sh, kf) + tn(se, kf)
        d_t[pl.ds(0, G), here] = (dq * scale).astype(BF)
        d_t[pl.ds(G, G), here] = (dk * scale).astype(BF)
        d_t[pl.ds(2 * G, G), here] = (dv * scale).astype(BF)

    HB = DB // 2

    def part(i):
        grads = d_t[:, pl.ds(i * C, C)]
        for b in range(NY):
            value = nn(w_all[pl.ds(b * DB, DB), :], grads).astype(BF)
            parts[i, b, 0] = value[:HB]
            parts[i, b, 1] = value[HB:]
        for n in range(2):
            y_copy(i, n).start()

    def y_own(i):
        for n in range(2, 4):
            y_copy(i, n).start()

    def y_copy(i, n):
        src, dst, dev = (
            (parts.at[i, y_far, 0], y_r1.at[i, 0], y_next),
            (parts.at[i, y_far, 1], y_r1.at[i, 1], y_prev),
            (parts.at[i, y_next, 1], y_r2.at[i, 0, 1], y_next),
            (parts.at[i, y_prev, 0], y_r2.at[i, 1, 0], y_prev),
            (parts.at[i, y_next, 0], y_r2.at[i, 0, 0], y_next),
            (parts.at[i, y_prev, 1], y_r2.at[i, 1, 1], y_prev),
        )[n]
        return remote(src, dst, y_s.at[0], y_r.at[i, 0 if n < 2 else 1], (me, dev))

    def y_relay(i):
        take(y_r1.at[i], y_r.at[i, 0])
        for n, dest, half in ((0, y_next, 0), (1, y_prev, 1)):
            parts[i, dest, half] = (
                parts[i, dest, half].astype(F32) + y_r1[i, half].astype(F32)
            ).astype(BF)
            y_copy(i, 4 + n).start()

    def y_final(i):
        take(y_r2.at[i], y_r.at[i, 1])
        total = parts[i, y].astype(F32) + y_r2[i, 0].astype(F32) + y_r2[i, 1].astype(F32)
        gi_buf[pl.ds(i * C, C), :] = total.reshape(DB, C).astype(BF).T
        out_copy(i).start()

    def out_copy(i):
        rows = pl.ds(i * C, C)
        return pltpu.make_async_copy(gi_buf.at[rows, :], gi_ref.at[rows, :], out_sem.at[0])

    def c_copy(w):
        return remote(
            wg.at[w, :, :, 1 - c], c_r.at[w], w_s.at[0], c_rs.at[w], sib
        )

    def weight(w):
        cols = d_t[pl.ds(w * G, G), :]

        span = D // 4
        per = NZ // 4 if NZ >= 4 else 0
        for i in range(4):
            value = nt(frt[pl.ds(i * span, span), :], cols).astype(BF)
            if per:
                wg[w, pl.ds(i * per, per)] = value.reshape(per, NX, NC, R, G)
            else:
                wg[w, i * NZ // 4, pl.ds((i % 2) * NX // 2, NX // 2)] = value.reshape(
                    NX // 2, NC, R, G
                )
        c_copy(w).start()

    x_next, x_prev, x_far = (lax.rem(x + d, NX) for d in (1, NX - 1, 2))

    def xw_copy(w, n):
        src, dst, dev = (
            (w_s1.at[w, x_far, 0], x_r1.at[w, 0], x_next),
            (w_s1.at[w, x_far, 1], x_r1.at[w, 1], x_prev),
            (w_s1.at[w, x_next, 1], x_r2.at[w, 0, 1], x_next),
            (w_s1.at[w, x_prev, 0], x_r2.at[w, 1, 0], x_prev),
            (w_s1.at[w, x_next, 0], x_r2.at[w, 0, 0], x_next),
            (w_s1.at[w, x_prev, 1], x_r2.at[w, 1, 1], x_prev),
        )[n]
        return remote(
            src, dst, w_s.at[1], w_r.at[w, 0 if n < 2 else 1], at(z, dev, c)
        )

    def w_core(w):
        c_copy(w).wait_recv()
        for b in range(NX):
            value = wg[w, :, b, c].astype(F32) + c_r[w, :, b].astype(F32)
            w_s1[w, b] = value.astype(BF).reshape(2, NZ // 2, R, G)
        for n in range(2):
            xw_copy(w, n).start()

    def w_own(w):
        for n in range(2, 4):
            xw_copy(w, n).start()

    def w_relay(w):
        take(x_r1.at[w], w_r.at[w, 0])
        for n, dest, half in ((0, x_next, 0), (1, x_prev, 1)):
            w_s1[w, dest, half] = (
                w_s1[w, dest, half].astype(F32) + x_r1[w, half].astype(F32)
            ).astype(BF)
            xw_copy(w, 4 + n).start()

    def wz_copy(w, d):
        zt = lax.rem(z + d, NZ)
        return remote(
            w_s2.at[w, zt], z_r.at[w, d - 1], w_s.at[2], wz_r.at[w],
            at(zt, x, c),
        )

    def w_cross(w):
        take(x_r2.at[w], w_r.at[w, 1])
        value = w_s1[w, x].astype(F32) + x_r2[w, 0].astype(F32) + x_r2[w, 1].astype(F32)
        value = value.reshape(NZ, R, G)
        w_s2f[w] = value
        w_s2[w] = value.astype(BF)
        for d in sorted(range(1, NZ), key=lambda n: -min(n, NZ - n)):
            wz_copy(w, d).start()

    def w_final(w):
        total = w_s2f[w, z]
        take(z_r.at[w], wz_r.at[w])
        for d in range(1, NZ):
            total = total + z_r[w, d - 1].astype(F32)
        gw_buf[w] = total
        gw_copy(w).start()

    def gw_copy(w):
        return pltpu.make_async_copy(
            gw_buf.at[w], (gwq_ref, gwk_ref, gwv_ref)[w], out_sem.at[0]
        )

    def y_drain():
        for i in range(NCH):
            out_copy(i).wait()
        for w in range(3):
            gw_copy(w).wait()
        scan1.wait_send()
        scan4.wait_send()
        for half in range(2):
            for d in range(1, NZ):
                @pl.when(zp + d < NZ)
                def _():
                    z_copy(half, d).wait_send()
            for d in range(1, NX):
                x_copy(half, d, sc_p.at[0]).wait_send()
        take(parts.at[:, pl.ds(0, 3)], y_s.at[0])
        take(c_r, w_s.at[0])
        take(w_s1.at[:, pl.ds(0, 3)], w_s.at[1])
        take(z_r, w_s.at[2])

    finish(0)
    part(0)
    y_own(0)
    finish(1)
    finish(2)
    finish(3)
    weight(0)
    part(1)
    weight(1)
    w_core(0)
    y_own(1)
    weight(2)
    part(2)
    w_core(1)
    w_own(0)
    y_relay(0)
    part(3)
    y_own(2)
    w_core(2)
    w_own(1)
    w_relay(0)
    w_own(2)
    w_relay(1)
    y_relay(1)
    y_own(3)
    w_relay(2)
    y_relay(2)
    w_cross(0)
    w_cross(1)
    y_relay(3)
    w_cross(2)
    y_final(0)
    y_final(1)
    w_final(0)
    w_final(1)
    y_final(2)
    w_final(2)
    y_final(3)
    y_drain()


def hand_over(a, b, c, d, oa, ob, oc, od, sem):
    copies = [
        pltpu.make_async_copy(src, dst, sem.at[n])
        for n, (src, dst) in enumerate(((a, oa), (b, ob), (c, oc), (d, od)))
    ]
    for copy in copies:
        copy.start()
    for copy in copies:
        copy.wait()


def build(mesh, interpret_dims=None):
    chunk, dh = interpret_dims or (CHUNK, DH)

    def local(frames, grad_out, w_query, w_key, w_value):
        T, D = frames.shape
        G = w_query.shape[1]
        NM, NY = mesh.shape["tm"], mesh.shape["head"]
        NZ = NM // (NX * NC)
        NH = G // dh
        C = chunk
        NCH = T // C
        R, DB = D // NM, D // NY
        HB = DB // 2
        dims = dict(T=T, D=D, G=G, C=C, NZ=NZ, NY=NY, NH=NH, DH=dh)
        V = pltpu.VMEM
        S = pltpu.SemaphoreType.DMA
        scratch = [
            V((T, D), BF), V((T, G), BF), V((D, 3 * G), BF), V((T, G), BF),
            V((G, T), BF), V((G, T), BF), V((G, T), BF), V((G, T), BF), V((D, T), BF),
            V((NCH, G, G), F32), V((NCH, G, G), F32),
            V((2, dh, G), F32), V((2, dh, G), BF),
            V((dh, G), BF), V((dh, G), F32), V((2, dh // 2, G), BF),
            V((2, NZ - 1, dh // 2, G), BF), V((dh, G), F32),
            V((3, dh // 2, G), BF), V((2, NX - 1, dh // 2, G), BF), V((dh, G), BF), V((dh, G), BF),
            V((2, dh, G), F32),
            V((3 * G, T), F32), V((3 * G, T), BF),
            V((NCH, NY, 2, HB, C), BF), V((NCH, 2, HB, C), BF), V((NCH, 2, 2, HB, C), BF),
            V((T, DB), BF), V((3, R, G), F32),
            V((3, NZ, NX, NC, R, G), BF), V((3, NZ, NX, R, G), BF),
            V((3, NX, 2, NZ // 2, R, G), BF), V((3, 2, NZ // 2, R, G), BF),
            V((3, 2, 2, NZ // 2, R, G), BF),
            V((3, NZ, R, G), BF), V((3, NZ, R, G), F32), V((3, NZ - 1, R, G), BF),
            S((4 + NCH,)), S((1,)), S((4,)), S((2,)), S((2, NZ - 1)), S((2, NX - 1)),
            S((1,)), S((NCH, 2)), S((3,)), S((3,)), S((3, 2)), S((3,)),
        ]
        anyspace = pl.BlockSpec(memory_space=pl.ANY)
        hbm = pl.BlockSpec(memory_space=pltpu.HBM)
        shapes = [
            jax.ShapeDtypeStruct((T, DB), BF),
            jax.ShapeDtypeStruct((R, G), F32),
            jax.ShapeDtypeStruct((R, G), F32),
            jax.ShapeDtypeStruct((R, G), F32),
        ]
        results = pl.pallas_call(
            functools.partial(kernel, dims),
            out_shape=shapes,
            in_specs=[hbm] * 5,
            out_specs=[anyspace] * 4,
            scratch_shapes=scratch,
            compiler_params=pltpu.CompilerParams(
                collective_id=0, has_side_effects=True, vmem_limit_bytes=48 * 2**20
            ),
        )(
            *[
                pltpu.with_memory_space_constraint(array, pltpu.HBM)
                for array in (frames, grad_out, w_query, w_key, w_value)
            ]
        )
        return pl.pallas_call(
            hand_over,
            out_shape=shapes,
            in_specs=[anyspace] * 4,
            out_specs=[hbm] * 4,
            scratch_shapes=[S((4,))],
            compiler_params=pltpu.CompilerParams(vmem_limit_bytes=4 * 2**20),
        )(*results)

    placed = (P("tm", None), P("tm", "head"), P(None, "head"), P(None, "head"), P(None, "head"))
    return jax.shard_map(
        local,
        mesh=mesh,
        in_specs=placed,
        out_specs=(P("tm", "head"), P("tm", "head"), P("tm", "head"), P("tm", "head")),
        check_vma=False,
    )


def solution(mesh):
    return build(mesh)
```

```python
import functools

import jax
import jax.numpy as jnp
from jax import lax
from jax.experimental import pallas as pl
from jax.experimental.pallas import tpu as pltpu
from jax.sharding import PartitionSpec as P

DH = 64
CHUNK = 256
NX = 4
NC = 2
MESH = pl.DeviceIdType.MESH
BF = jnp.bfloat16
F32 = jnp.float32


def nn(a, b):
    return lax.dot_general(a, b, (((1,), (0,)), ((), ())), preferred_element_type=F32)


def nt(a, b):
    return lax.dot_general(a, b, (((1,), (1,)), ((), ())), preferred_element_type=F32)


def tn(a, b):
    return lax.dot_general(a, b, (((0,), (0,)), ((), ())), preferred_element_type=F32)


def kernel(
    dims,
    frames_hbm, grad_hbm, wq_hbm, wk_hbm, wv_hbm,
    gi_ref, gwq_ref, gwk_ref, gwv_ref,
    fr, g_tok, w_all, q_tok, k_tok, v_tok, kt, vt, gt, frt,
    kvc, qgc, st, stb, sc_r1, sc_k, sc_zs, sc_zr, sc_acc, sc_p, sc_xr, sc_e, sc_r4, fin,
    d_in, d_t, parts, y_r1, y_r2,
    gi_buf, gw_buf, wg, c_r, w_s1, x_r1, x_r2, w_s2, w_s2f, z_r,
    in_sem, out_sem, sc_s, sc_rs, zs_r, xs_r, y_s, y_r, c_rs, w_s, w_r, wz_r,
):
    T, D, G, C, NZ, NY, NH, dh = (
        dims[k] for k in ("T", "D", "G", "C", "NZ", "NY", "NH", "DH")
    )
    NCH = T // C
    NM = NZ * NX * NC
    scale = float(dh * T * NM) ** (-0.5)
    R = D // NM
    DB = D // NY

    me = lax.axis_index("tm")
    y = lax.axis_index("head")
    c = lax.rem(me, NC)
    x = lax.rem(lax.div(me, NC), NX)
    z = lax.div(me, NC * NX)

    def at(zz, xx, cc, yy=None):
        return (zz * (NX * NC) + xx * NC + cc, y if yy is None else yy)

    sib = at(z, x, 1 - c)

    copies_in = [
        pltpu.make_async_copy(
            frames_hbm.at[pl.ds(i * C, C), :], fr.at[pl.ds(i * C, C), :], in_sem.at[4 + i]
        )
        for i in range(NCH)
    ]
    copies_w = [
        pltpu.make_async_copy(ref, w_all.at[:, pl.ds(i * G, G)], in_sem.at[i])
        for i, ref in enumerate((wq_hbm, wk_hbm, wv_hbm))
    ]
    copy_g = pltpu.make_async_copy(grad_hbm, g_tok, in_sem.at[3])
    for copy in copies_w:
        copy.start()
    for copy in copies_in:
        copy.start()
    copy_g.start()

    barrier = pltpu.get_barrier_semaphore()
    peers = [sib]
    peers += [at(lax.rem(z + d, NZ), x, c) for d in range(1, NZ)]
    peers += [at(z, lax.rem(x + d, NX), c) for d in range(1, NX)]
    y_next, y_prev, y_far = (lax.rem(y + d, NY) for d in (1, NY - 1, 2))
    peers += [(me, y_next), (me, y_prev)]
    for peer in peers:
        pl.semaphore_signal(barrier, inc=1, device_id=peer, device_id_type=MESH)

    row = lax.broadcasted_iota(jnp.int32, (G, G), 0)
    col = lax.broadcasted_iota(jnp.int32, (G, G), 1)
    same = lax.div(row, dh) == lax.div(col, dh)

    def spread(packed):
        return jnp.where(same, jnp.concatenate([packed] * NH, axis=0), 0.0)

    def pack(full):
        total = full[0:dh]
        for h in range(1, NH):
            total = total + full[h * dh : (h + 1) * dh]
        return total

    def chunk(i):
        return pl.ds(i * C, C)

    def project_one(w, out, i):
        out[chunk(i), :] = nn(fr[chunk(i), :], w_all[:, w * G : (w + 1) * G]).astype(BF)

    def state_one(left, right, out, i):
        out[i] = jnp.where(same, tn(left[chunk(i), :], right[chunk(i), :]), 0.0)

    def project_first():
        for copy in copies_w:
            copy.wait()
        copies_in[0].wait()
        project_one(1, k_tok, 0)
        project_one(2, v_tok, 0)
        project_one(0, q_tok, 0)

    def project_rest():
        for copy in copies_in[1:]:
            copy.wait()
        copy_g.wait()
        for w, out in ((1, k_tok), (2, v_tok), (0, q_tok)):
            for i in range(1, NCH):
                project_one(w, out, i)
        for i in range(NCH):
            state_one(k_tok, v_tok, kvc, i)
            state_one(q_tok, g_tok, qgc, i)

    project_first()
    project_rest()

    st[0] = pack(sum(kvc[i] for i in range(NCH)))
    st[1] = pack(sum(qgc[i] for i in range(NCH)))
    stb[...] = st[...].astype(BF)
    pl.semaphore_wait(barrier, len(peers))

    def remote(src, dst, send, recv, dev):
        return pltpu.make_async_remote_copy(
            src_ref=src, dst_ref=dst, send_sem=send, recv_sem=recv,
            device_id=dev, device_id_type=MESH,
        )

    def take(ref, sem):
        pltpu.make_async_copy(ref, ref, sem).wait()

    scan1 = remote(stb.at[1 - c], sc_r1, sc_s.at[0], sc_rs.at[0], sib)
    scan1.start()

    side = 1 - 2 * c
    zp = z + c * (NZ - 1 - 2 * z)
    xp = x + c * (NX - 1 - 2 * x)

    hd = dh // 2
    far_first = sorted(range(1, NZ), key=lambda n: -min(n, NZ - n))

    x_far_first = sorted(range(1, NX), key=lambda n: -min(n, NX - n))

    def z_copy(half, d):
        return remote(
            sc_zs.at[half], sc_zr.at[half, d - 1], sc_s.at[2], zs_r.at[half, d - 1],
            at(lax.rem(z + side * d + NZ, NZ), x, c),
        )

    def z_start(half):
        for d in far_first:
            @pl.when(zp + d < NZ)
            def _():
                z_copy(half, d).start()

    def z_gather(half):
        rows = pl.ds(half * hd, hd)
        for d in range(1, NZ):
            @pl.when(zp >= d)
            def _():
                z_copy(half, d).wait_recv()
                sc_acc[rows] += sc_zr[half, d - 1].astype(F32)

    def x_copy(half, d, src):
        return remote(
            src, sc_xr.at[half, d - 1], sc_s.at[3], xs_r.at[half, d - 1],
            at(z, lax.rem(x + d, NX), c),
        )

    def scan_start():
        scan1.wait_recv()
        chip = st[c] + sc_r1[...].astype(F32)
        sc_k[...] = chip
        sc_p[2] = chip[hd:].astype(BF)
        sc_zs[0] = chip[:hd].astype(BF)
        for d in x_far_first:
            x_copy(1, d, sc_p.at[2]).start()
        z_start(0)
        sc_acc[...] = jnp.zeros_like(sc_acc)

    def scan_mid_b():
        total = sc_k[pl.ds(hd, hd)]
        ahead = jnp.zeros_like(total)
        for d in range(1, NX):
            x_copy(1, d, sc_p.at[2]).wait_recv()
        for d in range(1, NX):
            xs = lax.rem(x + NX - d, NX)
            value = sc_xr[1, d - 1].astype(F32)
            total = total + value
            ahead = ahead + jnp.where(side * (x - xs) > 0, value, 0.0)
        sc_acc[pl.ds(hd, hd)] = ahead
        sc_zs[1] = total.astype(BF)
        z_start(1)

    def scan_mid_a():
        z_gather(0)
        own = sc_acc[pl.ds(0, hd)]
        sc_p[0] = own.astype(BF)
        sc_p[1] = (own + sc_k[pl.ds(0, hd)]).astype(BF)
        for d in x_far_first:
            xt = lax.rem(x + d, NX)
            later = jnp.where(side * (xt - x) > 0, 1, 0)
            x_copy(0, d, sc_p.at[later]).start()

    def scan_fin():
        for d in range(1, NX):
            x_copy(0, d, sc_p.at[0]).wait_recv()
        own = sc_acc[pl.ds(0, hd)]
        for d in range(1, NX):
            own = own + sc_xr[0, d - 1].astype(F32)
        sc_acc[pl.ds(0, hd)] = own
        z_gather(1)
        own = sc_acc[...]
        fin[c] = own
        sc_e[...] = (own + st[c]).astype(BF)
        scan4.start()

    scan4 = remote(sc_e, sc_r4, sc_s.at[1], sc_rs.at[1], sib)

    def scan_end():
        scan4.wait_recv()
        fin[1 - c] = sc_r4[...].astype(F32)

    tri = lax.broadcasted_iota(jnp.int32, (C, C), 0) >= lax.broadcasted_iota(
        jnp.int32, (C, C), 1
    )
    lane_head = lax.div(lax.broadcasted_iota(jnp.int32, (C, G), 1), dh)

    def intra(i):
        here = pl.ds(i * C, C)
        g = g_tok[here, :]
        q = q_tok[here, :]
        qf = q.T
        gf = g.T
        kf = k_tok[here, :].T
        vf = v_tok[here, :].T
        gt[:, here] = gf
        kt[:, here] = kf
        vt[:, here] = vf
        zero = jnp.zeros_like(g)
        for h in range(NH):
            rows = slice(h * dh, (h + 1) * dh)
            pg = nn(jnp.where(lane_head == h, g, zero), vf)
            pg = jnp.where(tri, pg, 0.0).astype(BF)
            sk = nn(jnp.where(lane_head == h, q, zero), kf)
            sk = jnp.where(tri, sk, 0.0).astype(BF)
            d_in[pl.ds(h * dh, dh), here] = nt(kf[rows], pg)
            d_in[pl.ds(G + h * dh, dh), here] = nn(qf[rows], pg)
            d_in[pl.ds(2 * G + h * dh, dh), here] = nn(gf[rows], sk)

    def flip(i):
        here = pl.ds(i * C, C)
        for b in range(D // C):
            frt[pl.ds(b * C, C), here] = fr[here, pl.ds(b * C, C)].T

    flip(0)
    flip(1)
    scan_start()
    intra(0)
    intra(1)
    scan_mid_b()
    intra(2)
    flip(2)
    scan_mid_a()
    intra(3)
    flip(3)
    scan_fin()
    scan_end()

    def finish(i):
        here = pl.ds(i * C, C)
        prefix = spread(fin[0])
        suffix = spread(fin[1])
        for j in range(i):
            prefix = prefix + kvc[j]
        for j in range(i + 1, NCH):
            suffix = suffix + qgc[j]
        prefix = prefix.astype(BF)
        suffix = suffix.astype(BF)
        kf, vf, gf = kt[:, here], vt[:, here], gt[:, here]
        dq = d_in[pl.ds(0, G), here] + nn(prefix, gf)
        dk = d_in[pl.ds(G, G), here] + nn(suffix, vf)
        dv = d_in[pl.ds(2 * G, G), here] + tn(suffix, kf)
        d_t[pl.ds(0, G), here] = (dq * scale).astype(BF)
        d_t[pl.ds(G, G), here] = (dk * scale).astype(BF)
        d_t[pl.ds(2 * G, G), here] = (dv * scale).astype(BF)

    HB = DB // 2

    def part(i):
        grads = d_t[:, pl.ds(i * C, C)]
        if i == 0:
            rows = pl.ds(pl.multiple_of(y_far * DB, DB), DB)
            value = nn(w_all[rows, :], grads).astype(BF)
            parts[i, y_far, 0] = value[:HB]
            parts[i, y_far, 1] = value[HB:]
            y_copy(i, 0).start()
            y_copy(i, 1).start()
            for d in (1, NY - 1, 0):
                b = lax.rem(y + d, NY)
                rows = pl.ds(pl.multiple_of(b * DB, DB), DB)
                value = nn(w_all[rows, :], grads).astype(BF)
                parts[i, b, 0] = value[:HB]
                parts[i, b, 1] = value[HB:]
            return
        for b in range(NY):
            value = nn(w_all[pl.ds(b * DB, DB), :], grads).astype(BF)
            parts[i, b, 0] = value[:HB]
            parts[i, b, 1] = value[HB:]
        for n in range(2):
            y_copy(i, n).start()

    def y_own(i):
        for n in range(2, 4):
            y_copy(i, n).start()

    def y_copy(i, n):
        src, dst, dev = (
            (parts.at[i, y_far, 0], y_r1.at[i, 0], y_next),
            (parts.at[i, y_far, 1], y_r1.at[i, 1], y_prev),
            (parts.at[i, y_next, 1], y_r2.at[i, 0, 1], y_next),
            (parts.at[i, y_prev, 0], y_r2.at[i, 1, 0], y_prev),
            (parts.at[i, y_next, 0], y_r2.at[i, 0, 0], y_next),
            (parts.at[i, y_prev, 1], y_r2.at[i, 1, 1], y_prev),
        )[n]
        return remote(src, dst, y_s.at[0], y_r.at[i, 0 if n < 2 else 1], (me, dev))

    def y_relay(i):
        take(y_r1.at[i], y_r.at[i, 0])
        for n, dest, half in ((0, y_next, 0), (1, y_prev, 1)):
            parts[i, dest, half] = (
                parts[i, dest, half].astype(F32) + y_r1[i, half].astype(F32)
            ).astype(BF)
            y_copy(i, 4 + n).start()

    def y_final(i):
        take(y_r2.at[i], y_r.at[i, 1])
        total = parts[i, y].astype(F32) + y_r2[i, 0].astype(F32) + y_r2[i, 1].astype(F32)
        gi_buf[pl.ds(i * C, C), :] = total.reshape(DB, C).astype(BF).T
        out_copy(i).start()

    def out_copy(i):
        rows = pl.ds(i * C, C)
        return pltpu.make_async_copy(gi_buf.at[rows, :], gi_ref.at[rows, :], out_sem.at[0])

    def c_copy(w):
        return remote(
            wg.at[w, :, :, 1 - c], c_r.at[w], w_s.at[0], c_rs.at[w], sib
        )

    def weight(w):
        cols = d_t[pl.ds(w * G, G), :]

        span = D // 4
        per = NZ // 4 if NZ >= 4 else 0
        for i in range(4):
            value = nt(frt[pl.ds(i * span, span), :], cols).astype(BF)
            if per:
                wg[w, pl.ds(i * per, per)] = value.reshape(per, NX, NC, R, G)
            else:
                wg[w, i * NZ // 4, pl.ds((i % 2) * NX // 2, NX // 2)] = value.reshape(
                    NX // 2, NC, R, G
                )
        c_copy(w).start()

    x_next, x_prev, x_far = (lax.rem(x + d, NX) for d in (1, NX - 1, 2))

    def xw_copy(w, n):
        src, dst, dev = (
            (w_s1.at[w, x_far, 0], x_r1.at[w, 0], x_next),
            (w_s1.at[w, x_far, 1], x_r1.at[w, 1], x_prev),
            (w_s1.at[w, x_next, 1], x_r2.at[w, 0, 1], x_next),
            (w_s1.at[w, x_prev, 0], x_r2.at[w, 1, 0], x_prev),
            (w_s1.at[w, x_next, 0], x_r2.at[w, 0, 0], x_next),
            (w_s1.at[w, x_prev, 1], x_r2.at[w, 1, 1], x_prev),
        )[n]
        return remote(
            src, dst, w_s.at[1], w_r.at[w, 0 if n < 2 else 1], at(z, dev, c)
        )

    def w_core(w):
        c_copy(w).wait_recv()
        for b in range(NX):
            value = wg[w, :, b, c].astype(F32) + c_r[w, :, b].astype(F32)
            w_s1[w, b] = value.astype(BF).reshape(2, NZ // 2, R, G)
        for n in range(2):
            xw_copy(w, n).start()

    def w_own(w):
        for n in range(2, 4):
            xw_copy(w, n).start()

    def w_relay(w):
        take(x_r1.at[w], w_r.at[w, 0])
        for n, dest, half in ((0, x_next, 0), (1, x_prev, 1)):
            w_s1[w, dest, half] = (
                w_s1[w, dest, half].astype(F32) + x_r1[w, half].astype(F32)
            ).astype(BF)
            xw_copy(w, 4 + n).start()

    def wz_copy(w, d):
        zt = lax.rem(z + d, NZ)
        return remote(
            w_s2.at[w, zt], z_r.at[w, d - 1], w_s.at[2], wz_r.at[w],
            at(zt, x, c),
        )

    def w_cross(w):
        take(x_r2.at[w], w_r.at[w, 1])
        value = w_s1[w, x].astype(F32) + x_r2[w, 0].astype(F32) + x_r2[w, 1].astype(F32)
        value = value.reshape(NZ, R, G)
        w_s2f[w] = value
        w_s2[w] = value.astype(BF)
        for d in sorted(range(1, NZ), key=lambda n: -min(n, NZ - n)):
            wz_copy(w, d).start()

    def w_final(w):
        total = w_s2f[w, z]
        take(z_r.at[w], wz_r.at[w])
        for d in range(1, NZ):
            total = total + z_r[w, d - 1].astype(F32)
        gw_buf[w] = total
        gw_copy(w).start()

    def gw_copy(w):
        return pltpu.make_async_copy(
            gw_buf.at[w], (gwq_ref, gwk_ref, gwv_ref)[w], out_sem.at[0]
        )

    def y_drain():
        for i in range(NCH):
            out_copy(i).wait()
        for w in range(3):
            gw_copy(w).wait()
        scan1.wait_send()
        scan4.wait_send()
        for half in range(2):
            for d in range(1, NZ):
                @pl.when(zp + d < NZ)
                def _():
                    z_copy(half, d).wait_send()
            for d in range(1, NX):
                x_copy(half, d, sc_p.at[0]).wait_send()
        take(parts.at[:, pl.ds(0, 3)], y_s.at[0])
        take(c_r, w_s.at[0])
        take(w_s1.at[:, pl.ds(0, 3)], w_s.at[1])
        take(z_r, w_s.at[2])

    finish(0)
    part(0)
    y_own(0)
    finish(1)
    finish(2)
    finish(3)
    weight(0)
    part(1)
    y_own(1)
    weight(1)
    weight(2)
    w_core(0)
    w_own(0)
    y_relay(0)
    part(2)
    w_core(1)
    part(3)
    y_own(2)
    w_core(2)
    w_own(1)
    w_relay(0)
    w_own(2)
    y_relay(1)
    y_own(3)
    w_relay(1)
    w_relay(2)
    w_cross(0)
    w_cross(1)
    y_relay(2)
    w_cross(2)
    y_relay(3)
    y_final(0)
    y_final(1)
    w_final(0)
    w_final(1)
    y_final(2)
    w_final(2)
    y_final(3)
    y_drain()


def hand_over(a, b, c, d, oa, ob, oc, od, sem):
    copies = [
        pltpu.make_async_copy(src, dst, sem.at[n])
        for n, (src, dst) in enumerate(((b, ob), (c, oc), (d, od)))
    ]
    step = a.shape[0] // 4
    for n in range(4):
        rows = pl.ds(n * step, step)
        copies.append(pltpu.make_async_copy(a.at[rows, :], oa.at[rows, :], sem.at[3 + n]))
    for copy in copies:
        copy.start()
    for copy in copies:
        copy.wait()


def build(mesh, interpret_dims=None):
    chunk, dh = interpret_dims or (CHUNK, DH)

    def local(frames, grad_out, w_query, w_key, w_value):
        T, D = frames.shape
        G = w_query.shape[1]
        NM, NY = mesh.shape["tm"], mesh.shape["head"]
        NZ = NM // (NX * NC)
        NH = G // dh
        C = chunk
        NCH = T // C
        R, DB = D // NM, D // NY
        HB = DB // 2
        dims = dict(T=T, D=D, G=G, C=C, NZ=NZ, NY=NY, NH=NH, DH=dh)
        V = pltpu.VMEM
        S = pltpu.SemaphoreType.DMA
        scratch = [
            V((T, D), BF), V((T, G), BF), V((D, 3 * G), BF),
            V((T, G), BF), V((T, G), BF), V((T, G), BF),
            V((G, T), BF), V((G, T), BF), V((G, T), BF), V((D, T), BF),
            V((NCH, G, G), F32), V((NCH, G, G), F32),
            V((2, dh, G), F32), V((2, dh, G), BF),
            V((dh, G), BF), V((dh, G), F32), V((2, dh // 2, G), BF),
            V((2, NZ - 1, dh // 2, G), BF), V((dh, G), F32),
            V((3, dh // 2, G), BF), V((2, NX - 1, dh // 2, G), BF), V((dh, G), BF), V((dh, G), BF),
            V((2, dh, G), F32),
            V((3 * G, T), F32), V((3 * G, T), BF),
            V((NCH, NY, 2, HB, C), BF), V((NCH, 2, HB, C), BF), V((NCH, 2, 2, HB, C), BF),
            V((T, DB), BF), V((3, R, G), F32),
            V((3, NZ, NX, NC, R, G), BF), V((3, NZ, NX, R, G), BF),
            V((3, NX, 2, NZ // 2, R, G), BF), V((3, 2, NZ // 2, R, G), BF),
            V((3, 2, 2, NZ // 2, R, G), BF),
            V((3, NZ, R, G), BF), V((3, NZ, R, G), F32), V((3, NZ - 1, R, G), BF),
            S((4 + NCH,)), S((1,)), S((4,)), S((2,)), S((2, NZ - 1)), S((2, NX - 1)),
            S((1,)), S((NCH, 2)), S((3,)), S((3,)), S((3, 2)), S((3,)),
        ]
        anyspace = pl.BlockSpec(memory_space=pl.ANY)
        hbm = pl.BlockSpec(memory_space=pltpu.HBM)
        shapes = [
            jax.ShapeDtypeStruct((T, DB), BF),
            jax.ShapeDtypeStruct((R, G), F32),
            jax.ShapeDtypeStruct((R, G), F32),
            jax.ShapeDtypeStruct((R, G), F32),
        ]
        results = pl.pallas_call(
            functools.partial(kernel, dims),
            out_shape=shapes,
            in_specs=[hbm] * 5,
            out_specs=[anyspace] * 4,
            scratch_shapes=scratch,
            compiler_params=pltpu.CompilerParams(
                collective_id=0, has_side_effects=True, vmem_limit_bytes=48 * 2**20
            ),
        )(
            *[
                pltpu.with_memory_space_constraint(array, pltpu.HBM)
                for array in (frames, grad_out, w_query, w_key, w_value)
            ]
        )
        return pl.pallas_call(
            hand_over,
            out_shape=shapes,
            in_specs=[anyspace] * 4,
            out_specs=[hbm] * 4,
            scratch_shapes=[S((7,))],
            compiler_params=pltpu.CompilerParams(vmem_limit_bytes=4 * 2**20),
        )(*results)

    placed = (P("tm", None), P("tm", "head"), P(None, "head"), P(None, "head"), P(None, "head"))
    return jax.shard_map(
        local,
        mesh=mesh,
        in_specs=placed,
        out_specs=(P("tm", "head"), P("tm", "head"), P("tm", "head"), P("tm", "head")),
        check_vma=False,
    )


def solution(mesh):
    return build(mesh)
```

```python
import functools

import jax
import jax.numpy as jnp
from jax import lax
from jax.experimental import pallas as pl
from jax.experimental.pallas import tpu as pltpu
from jax.sharding import PartitionSpec as P

DH = 64
CHUNK = 256
NX = 4
NC = 2
MESH = pl.DeviceIdType.MESH
BF = jnp.bfloat16
F32 = jnp.float32


def nn(a, b):
    return lax.dot_general(a, b, (((1,), (0,)), ((), ())), preferred_element_type=F32)


def nt(a, b):
    return lax.dot_general(a, b, (((1,), (1,)), ((), ())), preferred_element_type=F32)


def tn(a, b):
    return lax.dot_general(a, b, (((0,), (0,)), ((), ())), preferred_element_type=F32)


def kernel(
    dims,
    frames_hbm, grad_hbm, wq_hbm, wk_hbm, wv_hbm,
    gi_ref, gwq_ref, gwk_ref, gwv_ref,
    fr, g_tok, w_all, q_tok, k_tok, v_tok, kt, vt, gt, frt,
    kvc, qgc, st, stb, sc_r1, sc_k, sc_zs, sc_zr, sc_acc, sc_p, sc_xr, sc_e, sc_r4, fin,
    d_in, d_t, parts, y_r1, y_r2,
    gi_buf, gw_buf, wg, c_r, w_s1, x_r1, x_r2, w_s2, w_s2f, z_r,
    in_sem, out_sem, sc_s, sc_rs, zs_r, xs_r, y_s, y_r, c_rs, w_s, w_r, wz_r,
):
    T, D, G, C, NZ, NY, NH, dh = (
        dims[k] for k in ("T", "D", "G", "C", "NZ", "NY", "NH", "DH")
    )
    NCH = T // C
    NM = NZ * NX * NC
    scale = float(dh * T * NM) ** (-0.5)
    R = D // NM
    DB = D // NY

    me = lax.axis_index("tm")
    y = lax.axis_index("head")
    c = lax.rem(me, NC)
    x = lax.rem(lax.div(me, NC), NX)
    z = lax.div(me, NC * NX)

    def at(zz, xx, cc, yy=None):
        return (zz * (NX * NC) + xx * NC + cc, y if yy is None else yy)

    sib = at(z, x, 1 - c)

    copies_in = [
        pltpu.make_async_copy(
            frames_hbm.at[pl.ds(i * C, C), :], fr.at[pl.ds(i * C, C), :], in_sem.at[4 + i]
        )
        for i in range(NCH)
    ]
    copies_w = [
        pltpu.make_async_copy(ref, w_all.at[:, pl.ds(i * G, G)], in_sem.at[i])
        for i, ref in enumerate((wq_hbm, wk_hbm, wv_hbm))
    ]
    copy_g = pltpu.make_async_copy(grad_hbm, g_tok, in_sem.at[3])
    for copy in copies_w:
        copy.start()
    for copy in copies_in:
        copy.start()
    copy_g.start()

    barrier = pltpu.get_barrier_semaphore()
    peers = [sib]
    peers += [at(lax.rem(z + d, NZ), x, c) for d in range(1, NZ)]
    peers += [at(z, lax.rem(x + d, NX), c) for d in range(1, NX)]
    y_next, y_prev, y_far = (lax.rem(y + d, NY) for d in (1, NY - 1, 2))
    peers += [(me, y_next), (me, y_prev)]
    for peer in peers:
        pl.semaphore_signal(barrier, inc=1, device_id=peer, device_id_type=MESH)

    row = lax.broadcasted_iota(jnp.int32, (G, G), 0)
    col = lax.broadcasted_iota(jnp.int32, (G, G), 1)
    same = lax.div(row, dh) == lax.div(col, dh)

    def spread(packed):
        return jnp.where(same, jnp.concatenate([packed] * NH, axis=0), 0.0)

    def pack(full):
        total = full[0:dh]
        for h in range(1, NH):
            total = total + full[h * dh : (h + 1) * dh]
        return total

    def chunk(i):
        return pl.ds(i * C, C)

    def project_one(w, out, i):
        out[chunk(i), :] = nn(fr[chunk(i), :], w_all[:, w * G : (w + 1) * G]).astype(BF)

    def state_one(left, right, out, i):
        out[i] = jnp.where(same, tn(left[chunk(i), :], right[chunk(i), :]), 0.0)

    def project_first():
        for copy in copies_w:
            copy.wait()
        copies_in[0].wait()
        project_one(1, k_tok, 0)
        project_one(2, v_tok, 0)
        project_one(0, q_tok, 0)

    def project_rest():
        for copy in copies_in[1:]:
            copy.wait()
        copy_g.wait()
        for w, out in ((1, k_tok), (2, v_tok), (0, q_tok)):
            for i in range(1, NCH):
                project_one(w, out, i)
        for i in range(NCH):
            state_one(k_tok, v_tok, kvc, i)
            state_one(q_tok, g_tok, qgc, i)

    project_first()
    project_rest()

    st[0] = pack(sum(kvc[i] for i in range(NCH)))
    st[1] = pack(sum(qgc[i] for i in range(NCH)))
    stb[...] = st[...].astype(BF)
    pl.semaphore_wait(barrier, len(peers))

    def remote(src, dst, send, recv, dev):
        return pltpu.make_async_remote_copy(
            src_ref=src, dst_ref=dst, send_sem=send, recv_sem=recv,
            device_id=dev, device_id_type=MESH,
        )

    def take(ref, sem):
        pltpu.make_async_copy(ref, ref, sem).wait()

    scan1 = remote(stb.at[1 - c], sc_r1, sc_s.at[0], sc_rs.at[0], sib)
    scan1.start()

    side = 1 - 2 * c
    zp = z + c * (NZ - 1 - 2 * z)
    xp = x + c * (NX - 1 - 2 * x)

    hd = dh // 2
    far_first = sorted(range(1, NZ), key=lambda n: -min(n, NZ - n))

    x_far_first = sorted(range(1, NX), key=lambda n: -min(n, NX - n))

    def z_copy(half, d):
        return remote(
            sc_zs.at[half], sc_zr.at[half, d - 1], sc_s.at[2], zs_r.at[half, d - 1],
            at(lax.rem(z + side * d + NZ, NZ), x, c),
        )

    def z_start(half):
        for d in far_first:
            @pl.when(zp + d < NZ)
            def _():
                z_copy(half, d).start()

    def z_gather(half):
        rows = pl.ds(half * hd, hd)
        for d in range(1, NZ):
            @pl.when(zp >= d)
            def _():
                z_copy(half, d).wait_recv()
                sc_acc[rows] += sc_zr[half, d - 1].astype(F32)

    def x_copy(half, d, src):
        return remote(
            src, sc_xr.at[half, d - 1], sc_s.at[3], xs_r.at[half, d - 1],
            at(z, lax.rem(x + d, NX), c),
        )

    def scan_start():
        scan1.wait_recv()
        chip = st[c] + sc_r1[...].astype(F32)
        sc_k[...] = chip
        sc_p[2] = chip[hd:].astype(BF)
        sc_zs[0] = chip[:hd].astype(BF)
        for d in x_far_first:
            x_copy(1, d, sc_p.at[2]).start()
        z_start(0)
        sc_acc[...] = jnp.zeros_like(sc_acc)

    def scan_mid_b():
        total = sc_k[pl.ds(hd, hd)]
        ahead = jnp.zeros_like(total)
        for d in range(1, NX):
            x_copy(1, d, sc_p.at[2]).wait_recv()
        for d in range(1, NX):
            xs = lax.rem(x + NX - d, NX)
            value = sc_xr[1, d - 1].astype(F32)
            total = total + value
            ahead = ahead + jnp.where(side * (x - xs) > 0, value, 0.0)
        sc_acc[pl.ds(hd, hd)] = ahead
        sc_zs[1] = total.astype(BF)
        z_start(1)

    def scan_mid_a():
        z_gather(0)
        own = sc_acc[pl.ds(0, hd)]
        sc_p[0] = own.astype(BF)
        sc_p[1] = (own + sc_k[pl.ds(0, hd)]).astype(BF)
        for d in x_far_first:
            xt = lax.rem(x + d, NX)
            later = jnp.where(side * (xt - x) > 0, 1, 0)
            x_copy(0, d, sc_p.at[later]).start()

    def scan_fin():
        for d in range(1, NX):
            x_copy(0, d, sc_p.at[0]).wait_recv()
        own = sc_acc[pl.ds(0, hd)]
        for d in range(1, NX):
            own = own + sc_xr[0, d - 1].astype(F32)
        sc_acc[pl.ds(0, hd)] = own
        z_gather(1)
        own = sc_acc[...]
        fin[c] = own
        sc_e[...] = (own + st[c]).astype(BF)
        scan4.start()

    scan4 = remote(sc_e, sc_r4, sc_s.at[1], sc_rs.at[1], sib)

    def scan_end():
        scan4.wait_recv()
        fin[1 - c] = sc_r4[...].astype(F32)

    tri = lax.broadcasted_iota(jnp.int32, (C, C), 0) >= lax.broadcasted_iota(
        jnp.int32, (C, C), 1
    )
    lane_head = lax.div(lax.broadcasted_iota(jnp.int32, (C, G), 1), dh)

    def intra(i):
        here = pl.ds(i * C, C)
        g = g_tok[here, :]
        q = q_tok[here, :]
        qf = q.T
        gf = g.T
        kf = k_tok[here, :].T
        vf = v_tok[here, :].T
        gt[:, here] = gf
        kt[:, here] = kf
        vt[:, here] = vf
        zero = jnp.zeros_like(g)
        for h in range(NH):
            rows = slice(h * dh, (h + 1) * dh)
            pg = nn(jnp.where(lane_head == h, g, zero), vf)
            pg = jnp.where(tri, pg, 0.0).astype(BF)
            sk = nn(jnp.where(lane_head == h, q, zero), kf)
            sk = jnp.where(tri, sk, 0.0).astype(BF)
            d_in[pl.ds(h * dh, dh), here] = nt(kf[rows], pg)
            d_in[pl.ds(G + h * dh, dh), here] = nn(qf[rows], pg)
            d_in[pl.ds(2 * G + h * dh, dh), here] = nn(gf[rows], sk)

    def flip(i):
        here = pl.ds(i * C, C)
        for b in range(D // C):
            frt[pl.ds(b * C, C), here] = fr[here, pl.ds(b * C, C)].T

    flip(0)
    scan_start()
    intra(0)
    intra(1)
    scan_mid_b()
    scan_mid_a()
    intra(2)
    intra(3)
    flip(1)
    flip(2)
    flip(3)
    scan_fin()
    scan_end()

    def finish(i):
        here = pl.ds(i * C, C)
        prefix = spread(fin[0])
        suffix = spread(fin[1])
        for j in range(i):
            prefix = prefix + kvc[j]
        for j in range(i + 1, NCH):
            suffix = suffix + qgc[j]
        prefix = prefix.astype(BF)
        suffix = suffix.astype(BF)
        kf, vf, gf = kt[:, here], vt[:, here], gt[:, here]
        dq = d_in[pl.ds(0, G), here] + nn(prefix, gf)
        dk = d_in[pl.ds(G, G), here] + nn(suffix, vf)
        dv = d_in[pl.ds(2 * G, G), here] + tn(suffix, kf)
        d_t[pl.ds(0, G), here] = (dq * scale).astype(BF)
        d_t[pl.ds(G, G), here] = (dk * scale).astype(BF)
        d_t[pl.ds(2 * G, G), here] = (dv * scale).astype(BF)

    HB = DB // 2

    def part(i):
        grads = d_t[:, pl.ds(i * C, C)]
        if i == 0:
            rows = pl.ds(pl.multiple_of(y_far * DB, DB), DB)
            value = nn(w_all[rows, :], grads).astype(BF)
            parts[i, y_far, 0] = value[:HB]
            parts[i, y_far, 1] = value[HB:]
            y_copy(i, 0).start()
            y_copy(i, 1).start()
            for d in (1, NY - 1, 0):
                b = lax.rem(y + d, NY)
                rows = pl.ds(pl.multiple_of(b * DB, DB), DB)
                value = nn(w_all[rows, :], grads).astype(BF)
                parts[i, b, 0] = value[:HB]
                parts[i, b, 1] = value[HB:]
            return
        for b in range(NY):
            value = nn(w_all[pl.ds(b * DB, DB), :], grads).astype(BF)
            parts[i, b, 0] = value[:HB]
            parts[i, b, 1] = value[HB:]
        for n in range(2):
            y_copy(i, n).start()

    def y_own(i):
        for n in range(2, 4):
            y_copy(i, n).start()

    def y_copy(i, n):
        src, dst, dev = (
            (parts.at[i, y_far, 0], y_r1.at[i, 0], y_next),
            (parts.at[i, y_far, 1], y_r1.at[i, 1], y_prev),
            (parts.at[i, y_next, 1], y_r2.at[i, 0, 1], y_next),
            (parts.at[i, y_prev, 0], y_r2.at[i, 1, 0], y_prev),
            (parts.at[i, y_next, 0], y_r2.at[i, 0, 0], y_next),
            (parts.at[i, y_prev, 1], y_r2.at[i, 1, 1], y_prev),
        )[n]
        return remote(src, dst, y_s.at[0], y_r.at[i, 0 if n < 2 else 1], (me, dev))

    def y_relay(i):
        take(y_r1.at[i], y_r.at[i, 0])
        for n, dest, half in ((0, y_next, 0), (1, y_prev, 1)):
            parts[i, dest, half] = (
                parts[i, dest, half].astype(F32) + y_r1[i, half].astype(F32)
            ).astype(BF)
            y_copy(i, 4 + n).start()

    def y_final(i):
        take(y_r2.at[i], y_r.at[i, 1])
        total = parts[i, y].astype(F32) + y_r2[i, 0].astype(F32) + y_r2[i, 1].astype(F32)
        gi_buf[pl.ds(i * C, C), :] = total.reshape(DB, C).astype(BF).T
        out_copy(i).start()

    def out_copy(i):
        rows = pl.ds(i * C, C)
        return pltpu.make_async_copy(gi_buf.at[rows, :], gi_ref.at[rows, :], out_sem.at[0])

    def c_copy(w):
        return remote(
            wg.at[w, :, :, 1 - c], c_r.at[w], w_s.at[0], c_rs.at[w], sib
        )

    def weight(w):
        cols = d_t[pl.ds(w * G, G), :]

        span = D // 4
        per = NZ // 4 if NZ >= 4 else 0
        for i in range(4):
            value = nt(frt[pl.ds(i * span, span), :], cols).astype(BF)
            if per:
                wg[w, pl.ds(i * per, per)] = value.reshape(per, NX, NC, R, G)
            else:
                wg[w, i * NZ // 4, pl.ds((i % 2) * NX // 2, NX // 2)] = value.reshape(
                    NX // 2, NC, R, G
                )
        c_copy(w).start()

    x_next, x_prev, x_far = (lax.rem(x + d, NX) for d in (1, NX - 1, 2))

    def xw_copy(w, n):
        src, dst, dev = (
            (w_s1.at[w, x_far, 0], x_r1.at[w, 0], x_next),
            (w_s1.at[w, x_far, 1], x_r1.at[w, 1], x_prev),
            (w_s1.at[w, x_next, 1], x_r2.at[w, 0, 1], x_next),
            (w_s1.at[w, x_prev, 0], x_r2.at[w, 1, 0], x_prev),
            (w_s1.at[w, x_next, 0], x_r2.at[w, 0, 0], x_next),
            (w_s1.at[w, x_prev, 1], x_r2.at[w, 1, 1], x_prev),
        )[n]
        return remote(
            src, dst, w_s.at[1], w_r.at[w, 0 if n < 2 else 1], at(z, dev, c)
        )

    def w_core(w):
        c_copy(w).wait_recv()
        for b in range(NX):
            value = wg[w, :, b, c].astype(F32) + c_r[w, :, b].astype(F32)
            w_s1[w, b] = value.astype(BF).reshape(2, NZ // 2, R, G)
        for n in range(2):
            xw_copy(w, n).start()

    def w_own(w):
        for n in range(2, 4):
            xw_copy(w, n).start()

    def w_relay(w):
        take(x_r1.at[w], w_r.at[w, 0])
        for n, dest, half in ((0, x_next, 0), (1, x_prev, 1)):
            w_s1[w, dest, half] = (
                w_s1[w, dest, half].astype(F32) + x_r1[w, half].astype(F32)
            ).astype(BF)
            xw_copy(w, 4 + n).start()

    def wz_copy(w, d):
        zt = lax.rem(z + d, NZ)
        return remote(
            w_s2.at[w, zt], z_r.at[w, d - 1], w_s.at[2], wz_r.at[w],
            at(zt, x, c),
        )

    def w_cross(w):
        take(x_r2.at[w], w_r.at[w, 1])
        value = w_s1[w, x].astype(F32) + x_r2[w, 0].astype(F32) + x_r2[w, 1].astype(F32)
        value = value.reshape(NZ, R, G)
        w_s2f[w] = value
        w_s2[w] = value.astype(BF)
        for d in sorted(range(1, NZ), key=lambda n: -min(n, NZ - n)):
            wz_copy(w, d).start()

    def w_final(w):
        total = w_s2f[w, z]
        take(z_r.at[w], wz_r.at[w])
        for d in range(1, NZ):
            total = total + z_r[w, d - 1].astype(F32)
        gw_buf[w] = total
        gw_copy(w).start()

    def gw_copy(w):
        return pltpu.make_async_copy(
            gw_buf.at[w], (gwq_ref, gwk_ref, gwv_ref)[w], out_sem.at[0]
        )

    def y_drain():
        for i in range(NCH):
            out_copy(i).wait()
        for w in range(3):
            gw_copy(w).wait()
        scan1.wait_send()
        scan4.wait_send()
        for half in range(2):
            for d in range(1, NZ):
                @pl.when(zp + d < NZ)
                def _():
                    z_copy(half, d).wait_send()
            for d in range(1, NX):
                x_copy(half, d, sc_p.at[0]).wait_send()
        take(parts.at[:, pl.ds(0, 3)], y_s.at[0])
        take(c_r, w_s.at[0])
        take(w_s1.at[:, pl.ds(0, 3)], w_s.at[1])
        take(z_r, w_s.at[2])

    finish(0)
    part(0)
    y_own(0)
    finish(1)
    finish(2)
    finish(3)
    weight(0)
    part(1)
    y_own(1)
    weight(1)
    weight(2)
    w_core(0)
    w_own(0)
    y_relay(0)
    part(2)
    w_core(1)
    part(3)
    y_own(2)
    w_core(2)
    w_own(1)
    w_relay(0)
    w_own(2)
    y_relay(1)
    y_own(3)
    w_relay(1)
    w_relay(2)
    w_cross(0)
    w_cross(1)
    y_relay(2)
    w_cross(2)
    y_relay(3)
    y_final(0)
    y_final(1)
    w_final(0)
    w_final(1)
    y_final(2)
    w_final(2)
    y_final(3)
    y_drain()


def hand_over(a, b, c, d, oa, ob, oc, od, sem):
    copies = [
        pltpu.make_async_copy(src, dst, sem.at[n])
        for n, (src, dst) in enumerate(((b, ob), (c, oc), (d, od)))
    ]
    step = a.shape[0] // 4
    for n in range(4):
        rows = pl.ds(n * step, step)
        copies.append(pltpu.make_async_copy(a.at[rows, :], oa.at[rows, :], sem.at[3 + n]))
    for copy in copies:
        copy.start()
    for copy in copies:
        copy.wait()


def build(mesh, interpret_dims=None):
    chunk, dh = interpret_dims or (CHUNK, DH)

    def local(frames, grad_out, w_query, w_key, w_value):
        T, D = frames.shape
        G = w_query.shape[1]
        NM, NY = mesh.shape["tm"], mesh.shape["head"]
        NZ = NM // (NX * NC)
        NH = G // dh
        C = chunk
        NCH = T // C
        R, DB = D // NM, D // NY
        HB = DB // 2
        dims = dict(T=T, D=D, G=G, C=C, NZ=NZ, NY=NY, NH=NH, DH=dh)
        V = pltpu.VMEM
        S = pltpu.SemaphoreType.DMA
        scratch = [
            V((T, D), BF), V((T, G), BF), V((D, 3 * G), BF),
            V((T, G), BF), V((T, G), BF), V((T, G), BF),
            V((G, T), BF), V((G, T), BF), V((G, T), BF), V((D, T), BF),
            V((NCH, G, G), F32), V((NCH, G, G), F32),
            V((2, dh, G), F32), V((2, dh, G), BF),
            V((dh, G), BF), V((dh, G), F32), V((2, dh // 2, G), BF),
            V((2, NZ - 1, dh // 2, G), BF), V((dh, G), F32),
            V((3, dh // 2, G), BF), V((2, NX - 1, dh // 2, G), BF), V((dh, G), BF), V((dh, G), BF),
            V((2, dh, G), F32),
            V((3 * G, T), F32), V((3 * G, T), BF),
            V((NCH, NY, 2, HB, C), BF), V((NCH, 2, HB, C), BF), V((NCH, 2, 2, HB, C), BF),
            V((T, DB), BF), V((3, R, G), F32),
            V((3, NZ, NX, NC, R, G), BF), V((3, NZ, NX, R, G), BF),
            V((3, NX, 2, NZ // 2, R, G), BF), V((3, 2, NZ // 2, R, G), BF),
            V((3, 2, 2, NZ // 2, R, G), BF),
            V((3, NZ, R, G), BF), V((3, NZ, R, G), F32), V((3, NZ - 1, R, G), BF),
            S((4 + NCH,)), S((1,)), S((4,)), S((2,)), S((2, NZ - 1)), S((2, NX - 1)),
            S((1,)), S((NCH, 2)), S((3,)), S((3,)), S((3, 2)), S((3,)),
        ]
        anyspace = pl.BlockSpec(memory_space=pl.ANY)
        hbm = pl.BlockSpec(memory_space=pltpu.HBM)
        shapes = [
            jax.ShapeDtypeStruct((T, DB), BF),
            jax.ShapeDtypeStruct((R, G), F32),
            jax.ShapeDtypeStruct((R, G), F32),
            jax.ShapeDtypeStruct((R, G), F32),
        ]
        results = pl.pallas_call(
            functools.partial(kernel, dims),
            out_shape=shapes,
            in_specs=[hbm] * 5,
            out_specs=[anyspace] * 4,
            scratch_shapes=scratch,
            compiler_params=pltpu.CompilerParams(
                collective_id=0, has_side_effects=True, vmem_limit_bytes=48 * 2**20
            ),
        )(
            *[
                pltpu.with_memory_space_constraint(array, pltpu.HBM)
                for array in (frames, grad_out, w_query, w_key, w_value)
            ]
        )
        return pl.pallas_call(
            hand_over,
            out_shape=shapes,
            in_specs=[anyspace] * 4,
            out_specs=[hbm] * 4,
            scratch_shapes=[S((7,))],
            compiler_params=pltpu.CompilerParams(vmem_limit_bytes=4 * 2**20),
        )(*results)

    placed = (P("tm", None), P("tm", "head"), P(None, "head"), P(None, "head"), P(None, "head"))
    return jax.shard_map(
        local,
        mesh=mesh,
        in_specs=placed,
        out_specs=(P("tm", "head"), P("tm", "head"), P("tm", "head"), P("tm", "head")),
        check_vma=False,
    )


def solution(mesh):
    return build(mesh)
```

```python
import functools

import jax
import jax.numpy as jnp
from jax import lax
from jax.experimental import pallas as pl
from jax.experimental.pallas import tpu as pltpu
from jax.sharding import PartitionSpec as P

DH = 64
CHUNK = 256
NX = 4
NC = 2
MESH = pl.DeviceIdType.MESH
BF = jnp.bfloat16
F32 = jnp.float32


def nn(a, b):
    return lax.dot_general(a, b, (((1,), (0,)), ((), ())), preferred_element_type=F32)


def nt(a, b):
    return lax.dot_general(a, b, (((1,), (1,)), ((), ())), preferred_element_type=F32)


def tn(a, b):
    return lax.dot_general(a, b, (((0,), (0,)), ((), ())), preferred_element_type=F32)


def kernel(
    dims,
    frames_hbm, grad_hbm, wq_hbm, wk_hbm, wv_hbm,
    gi_ref, gwq_ref, gwk_ref, gwv_ref,
    fr, g_tok, w_all, q_tok, k_tok, v_tok, kt, vt, gt, frt,
    kvc, qgc, st, stb, sc_r1, sc_k, sc_zs, sc_zr, sc_acc, sc_p, sc_xr, sc_e, sc_r4, fin,
    d_in, d_t, parts, y_r1, y_r2,
    gi_buf, gw_buf, wg, c_r, w_s1, x_r1, x_r2, w_s2, w_s2f, z_r,
    in_sem, out_sem, sc_s, sc_rs, zs_r, xs_r, y_s, y_r, c_rs, w_s, w_r, wz_r,
):
    T, D, G, C, NZ, NY, NH, dh = (
        dims[k] for k in ("T", "D", "G", "C", "NZ", "NY", "NH", "DH")
    )
    NCH = T // C
    NM = NZ * NX * NC
    scale = float(dh * T * NM) ** (-0.5)
    R = D // NM
    DB = D // NY

    me = lax.axis_index("tm")
    y = lax.axis_index("head")
    c = lax.rem(me, NC)
    x = lax.rem(lax.div(me, NC), NX)
    z = lax.div(me, NC * NX)

    def at(zz, xx, cc, yy=None):
        return (zz * (NX * NC) + xx * NC + cc, y if yy is None else yy)

    sib = at(z, x, 1 - c)

    copies_in = [
        pltpu.make_async_copy(
            frames_hbm.at[pl.ds(i * C, C), :], fr.at[pl.ds(i * C, C), :], in_sem.at[4 + i]
        )
        for i in range(NCH)
    ]
    copies_w = [
        pltpu.make_async_copy(ref, w_all.at[:, pl.ds(i * G, G)], in_sem.at[i])
        for i, ref in enumerate((wq_hbm, wk_hbm, wv_hbm))
    ]
    copy_g = pltpu.make_async_copy(grad_hbm, g_tok, in_sem.at[3])
    for copy in copies_w:
        copy.start()
    for copy in copies_in:
        copy.start()
    copy_g.start()

    barrier = pltpu.get_barrier_semaphore()
    peers = [sib]
    peers += [at(lax.rem(z + d, NZ), x, c) for d in range(1, NZ)]
    peers += [at(z, lax.rem(x + d, NX), c) for d in range(1, NX)]
    y_next, y_prev, y_far = (lax.rem(y + d, NY) for d in (1, NY - 1, 2))
    peers += [(me, y_next), (me, y_prev)]
    for peer in peers:
        pl.semaphore_signal(barrier, inc=1, device_id=peer, device_id_type=MESH)

    row = lax.broadcasted_iota(jnp.int32, (G, G), 0)
    col = lax.broadcasted_iota(jnp.int32, (G, G), 1)
    same = lax.div(row, dh) == lax.div(col, dh)

    def spread(packed):
        return jnp.where(same, jnp.concatenate([packed] * NH, axis=0), 0.0)

    def pack(full):
        total = full[0:dh]
        for h in range(1, NH):
            total = total + full[h * dh : (h + 1) * dh]
        return total

    def chunk(i):
        return pl.ds(i * C, C)

    def project_one(w, out, i):
        out[chunk(i), :] = nn(fr[chunk(i), :], w_all[:, w * G : (w + 1) * G]).astype(BF)

    def state_one(left, right, out, i):
        out[i] = jnp.where(same, tn(left[chunk(i), :], right[chunk(i), :]), 0.0)

    def project_first():
        for copy in copies_w:
            copy.wait()
        copies_in[0].wait()
        project_one(1, k_tok, 0)
        project_one(2, v_tok, 0)
        project_one(0, q_tok, 0)

    def project_rest():
        for copy in copies_in[1:]:
            copy.wait()
        copy_g.wait()
        for w, out in ((1, k_tok), (2, v_tok), (0, q_tok)):
            for i in range(1, NCH):
                project_one(w, out, i)
        for i in range(NCH):
            state_one(k_tok, v_tok, kvc, i)
            state_one(q_tok, g_tok, qgc, i)

    project_first()
    project_rest()

    st[0] = pack(sum(kvc[i] for i in range(NCH)))
    st[1] = pack(sum(qgc[i] for i in range(NCH)))
    stb[...] = st[...].astype(BF)
    pl.semaphore_wait(barrier, len(peers))

    def remote(src, dst, send, recv, dev):
        return pltpu.make_async_remote_copy(
            src_ref=src, dst_ref=dst, send_sem=send, recv_sem=recv,
            device_id=dev, device_id_type=MESH,
        )

    def take(ref, sem):
        pltpu.make_async_copy(ref, ref, sem).wait()

    scan1 = remote(stb.at[1 - c], sc_r1, sc_s.at[0], sc_rs.at[0], sib)
    scan1.start()

    side = 1 - 2 * c
    zp = z + c * (NZ - 1 - 2 * z)
    xp = x + c * (NX - 1 - 2 * x)

    hd = dh // 2
    far_first = sorted(range(1, NZ), key=lambda n: -min(n, NZ - n))

    x_far_first = sorted(range(1, NX), key=lambda n: -min(n, NX - n))

    def z_copy(half, d):
        return remote(
            sc_zs.at[half], sc_zr.at[half, d - 1], sc_s.at[2], zs_r.at[half, d - 1],
            at(lax.rem(z + side * d + NZ, NZ), x, c),
        )

    def z_start(half):
        for d in far_first:
            @pl.when(zp + d < NZ)
            def _():
                z_copy(half, d).start()

    def z_gather(half):
        rows = pl.ds(half * hd, hd)
        for d in range(1, NZ):
            @pl.when(zp >= d)
            def _():
                z_copy(half, d).wait_recv()
                sc_acc[rows] += sc_zr[half, d - 1].astype(F32)

    def x_copy(half, d, src):
        return remote(
            src, sc_xr.at[half, d - 1], sc_s.at[3], xs_r.at[half],
            at(z, lax.rem(x + d, NX), c),
        )

    def scan_start():
        scan1.wait_recv()
        chip = st[c] + sc_r1[...].astype(F32)
        sc_k[...] = chip
        sc_p[2] = chip[hd:].astype(BF)
        sc_zs[0] = chip[:hd].astype(BF)
        for d in x_far_first:
            x_copy(1, d, sc_p.at[2]).start()
        z_start(0)
        sc_acc[...] = jnp.zeros_like(sc_acc)

    def scan_mid_b():
        total = sc_k[pl.ds(hd, hd)]
        ahead = jnp.zeros_like(total)
        take(sc_xr.at[1], xs_r.at[1])
        for d in range(1, NX):
            xs = lax.rem(x + NX - d, NX)
            value = sc_xr[1, d - 1].astype(F32)
            total = total + value
            ahead = ahead + jnp.where(side * (x - xs) > 0, value, 0.0)
        sc_acc[pl.ds(hd, hd)] = ahead
        sc_zs[1] = total.astype(BF)
        z_start(1)

    def scan_mid_a():
        z_gather(0)
        own = sc_acc[pl.ds(0, hd)]
        sc_p[0] = own.astype(BF)
        sc_p[1] = (own + sc_k[pl.ds(0, hd)]).astype(BF)
        for d in x_far_first:
            xt = lax.rem(x + d, NX)
            later = jnp.where(side * (xt - x) > 0, 1, 0)
            x_copy(0, d, sc_p.at[later]).start()

    def scan_fin():
        take(sc_xr.at[0], xs_r.at[0])
        own = sc_acc[pl.ds(0, hd)]
        for d in range(1, NX):
            own = own + sc_xr[0, d - 1].astype(F32)
        sc_acc[pl.ds(0, hd)] = own
        z_gather(1)
        own = sc_acc[...]
        fin[c] = own
        sc_e[...] = (own + st[c]).astype(BF)
        scan4.start()

    scan4 = remote(sc_e, sc_r4, sc_s.at[1], sc_rs.at[1], sib)

    def scan_end():
        scan4.wait_recv()
        fin[1 - c] = sc_r4[...].astype(F32)

    tri = lax.broadcasted_iota(jnp.int32, (C, C), 0) >= lax.broadcasted_iota(
        jnp.int32, (C, C), 1
    )
    lane_head = lax.div(lax.broadcasted_iota(jnp.int32, (C, G), 1), dh)

    def intra(i):
        here = pl.ds(i * C, C)
        g = g_tok[here, :]
        q = q_tok[here, :]
        qf = q.T
        gf = g.T
        kf = k_tok[here, :].T
        vf = v_tok[here, :].T
        gt[:, here] = gf
        kt[:, here] = kf
        vt[:, here] = vf
        zero = jnp.zeros_like(g)
        for h in range(NH):
            rows = slice(h * dh, (h + 1) * dh)
            pg = nn(jnp.where(lane_head == h, g, zero), vf)
            pg = jnp.where(tri, pg, 0.0).astype(BF)
            sk = nn(jnp.where(lane_head == h, q, zero), kf)
            sk = jnp.where(tri, sk, 0.0).astype(BF)
            d_in[pl.ds(h * dh, dh), here] = nt(kf[rows], pg)
            d_in[pl.ds(G + h * dh, dh), here] = nn(qf[rows], pg)
            d_in[pl.ds(2 * G + h * dh, dh), here] = nn(gf[rows], sk)

    def flip(i):
        here = pl.ds(i * C, C)
        for b in range(D // C):
            frt[pl.ds(b * C, C), here] = fr[here, pl.ds(b * C, C)].T

    flip(0)
    scan_start()
    intra(0)
    intra(1)
    scan_mid_b()
    scan_mid_a()
    intra(2)
    intra(3)
    flip(1)
    flip(2)
    flip(3)
    scan_fin()
    scan_end()

    def finish(i):
        here = pl.ds(i * C, C)
        prefix = spread(fin[0])
        suffix = spread(fin[1])
        for j in range(i):
            prefix = prefix + kvc[j]
        for j in range(i + 1, NCH):
            suffix = suffix + qgc[j]
        prefix = prefix.astype(BF)
        suffix = suffix.astype(BF)
        kf, vf, gf = kt[:, here], vt[:, here], gt[:, here]
        dq = d_in[pl.ds(0, G), here] + nn(prefix, gf)
        dk = d_in[pl.ds(G, G), here] + nn(suffix, vf)
        dv = d_in[pl.ds(2 * G, G), here] + tn(suffix, kf)
        d_t[pl.ds(0, G), here] = (dq * scale).astype(BF)
        d_t[pl.ds(G, G), here] = (dk * scale).astype(BF)
        d_t[pl.ds(2 * G, G), here] = (dv * scale).astype(BF)

    HB = DB // 2

    def part(i):
        grads = d_t[:, pl.ds(i * C, C)]
        if i == 0:
            rows = pl.ds(pl.multiple_of(y_far * DB, DB), DB)
            value = nn(w_all[rows, :], grads).astype(BF)
            parts[i, y_far, 0] = value[:HB]
            parts[i, y_far, 1] = value[HB:]
            y_copy(i, 0).start()
            y_copy(i, 1).start()
            for d in (1, NY - 1, 0):
                b = lax.rem(y + d, NY)
                rows = pl.ds(pl.multiple_of(b * DB, DB), DB)
                value = nn(w_all[rows, :], grads).astype(BF)
                parts[i, b, 0] = value[:HB]
                parts[i, b, 1] = value[HB:]
            return
        for b in range(NY):
            value = nn(w_all[pl.ds(b * DB, DB), :], grads).astype(BF)
            parts[i, b, 0] = value[:HB]
            parts[i, b, 1] = value[HB:]
        for n in range(2):
            y_copy(i, n).start()

    def y_own(i):
        for n in range(2, 4):
            y_copy(i, n).start()

    def y_copy(i, n):
        src, dst, dev = (
            (parts.at[i, y_far, 0], y_r1.at[i, 0], y_next),
            (parts.at[i, y_far, 1], y_r1.at[i, 1], y_prev),
            (parts.at[i, y_next, 1], y_r2.at[i, 0, 1], y_next),
            (parts.at[i, y_prev, 0], y_r2.at[i, 1, 0], y_prev),
            (parts.at[i, y_next, 0], y_r2.at[i, 0, 0], y_next),
            (parts.at[i, y_prev, 1], y_r2.at[i, 1, 1], y_prev),
        )[n]
        return remote(src, dst, y_s.at[0], y_r.at[i, 0 if n < 2 else 1], (me, dev))

    def y_relay(i):
        take(y_r1.at[i], y_r.at[i, 0])
        for n, dest, half in ((0, y_next, 0), (1, y_prev, 1)):
            parts[i, dest, half] = (
                parts[i, dest, half].astype(F32) + y_r1[i, half].astype(F32)
            ).astype(BF)
            y_copy(i, 4 + n).start()

    def y_final(i):
        take(y_r2.at[i], y_r.at[i, 1])
        total = parts[i, y].astype(F32) + y_r2[i, 0].astype(F32) + y_r2[i, 1].astype(F32)
        gi_buf[pl.ds(i * C, C), :] = total.reshape(DB, C).astype(BF).T
        out_copy(i).start()

    def out_copy(i):
        rows = pl.ds(i * C, C)
        return pltpu.make_async_copy(gi_buf.at[rows, :], gi_ref.at[rows, :], out_sem.at[0])

    def c_copy(w):
        return remote(
            wg.at[w, :, :, 1 - c], c_r.at[w], w_s.at[0], c_rs.at[w], sib
        )

    def weight(w):
        cols = d_t[pl.ds(w * G, G), :]

        span = D // 4
        per = NZ // 4 if NZ >= 4 else 0
        for i in range(4):
            value = nt(frt[pl.ds(i * span, span), :], cols).astype(BF)
            if per:
                wg[w, pl.ds(i * per, per)] = value.reshape(per, NX, NC, R, G)
            else:
                wg[w, i * NZ // 4, pl.ds((i % 2) * NX // 2, NX // 2)] = value.reshape(
                    NX // 2, NC, R, G
                )
        c_copy(w).start()

    x_next, x_prev, x_far = (lax.rem(x + d, NX) for d in (1, NX - 1, 2))

    def xw_copy(w, n):
        src, dst, dev = (
            (w_s1.at[w, x_far, 0], x_r1.at[w, 0], x_next),
            (w_s1.at[w, x_far, 1], x_r1.at[w, 1], x_prev),
            (w_s1.at[w, x_next, 1], x_r2.at[w, 0, 1], x_next),
            (w_s1.at[w, x_prev, 0], x_r2.at[w, 1, 0], x_prev),
            (w_s1.at[w, x_next, 0], x_r2.at[w, 0, 0], x_next),
            (w_s1.at[w, x_prev, 1], x_r2.at[w, 1, 1], x_prev),
        )[n]
        return remote(
            src, dst, w_s.at[1], w_r.at[w, 0 if n < 2 else 1], at(z, dev, c)
        )

    def w_core(w):
        c_copy(w).wait_recv()
        for b in range(NX):
            value = wg[w, :, b, c].astype(F32) + c_r[w, :, b].astype(F32)
            w_s1[w, b] = value.astype(BF).reshape(2, NZ // 2, R, G)
        for n in range(2):
            xw_copy(w, n).start()

    def w_own(w):
        for n in range(2, 4):
            xw_copy(w, n).start()

    def w_relay(w):
        take(x_r1.at[w], w_r.at[w, 0])
        for n, dest, half in ((0, x_next, 0), (1, x_prev, 1)):
            w_s1[w, dest, half] = (
                w_s1[w, dest, half].astype(F32) + x_r1[w, half].astype(F32)
            ).astype(BF)
            xw_copy(w, 4 + n).start()

    def wz_copy(w, d):
        zt = lax.rem(z + d, NZ)
        return remote(
            w_s2.at[w, zt], z_r.at[w, d - 1], w_s.at[2], wz_r.at[w],
            at(zt, x, c),
        )

    def w_cross(w):
        take(x_r2.at[w], w_r.at[w, 1])
        value = w_s1[w, x].astype(F32) + x_r2[w, 0].astype(F32) + x_r2[w, 1].astype(F32)
        value = value.reshape(NZ, R, G)
        w_s2f[w] = value
        w_s2[w] = value.astype(BF)
        for d in sorted(range(1, NZ), key=lambda n: -min(n, NZ - n)):
            wz_copy(w, d).start()

    def w_final(w):
        total = w_s2f[w, z]
        take(z_r.at[w], wz_r.at[w])
        for d in range(1, NZ):
            total = total + z_r[w, d - 1].astype(F32)
        gw_buf[w] = total
        gw_copy(w).start()

    def gw_copy(w):
        return pltpu.make_async_copy(
            gw_buf.at[w], (gwq_ref, gwk_ref, gwv_ref)[w], out_sem.at[0]
        )

    def y_drain():
        for i in range(NCH):
            out_copy(i).wait()
        for w in range(3):
            gw_copy(w).wait()
        scan1.wait_send()
        scan4.wait_send()
        for half in range(2):
            for d in range(1, NZ):
                @pl.when(zp + d < NZ)
                def _():
                    z_copy(half, d).wait_send()
            take(sc_xr.at[half], sc_s.at[3])
        take(parts.at[:, pl.ds(0, 3)], y_s.at[0])
        take(c_r, w_s.at[0])
        take(w_s1.at[:, pl.ds(0, 3)], w_s.at[1])
        take(z_r, w_s.at[2])

    finish(0)
    part(0)
    y_own(0)
    finish(1)
    finish(2)
    finish(3)
    weight(0)
    part(1)
    y_own(1)
    weight(1)
    weight(2)
    w_core(0)
    w_own(0)
    y_relay(0)
    part(2)
    w_core(1)
    part(3)
    y_own(2)
    w_core(2)
    w_own(1)
    w_relay(0)
    w_own(2)
    y_relay(1)
    y_own(3)
    w_relay(1)
    w_relay(2)
    w_cross(0)
    w_cross(1)
    y_relay(2)
    w_cross(2)
    y_relay(3)
    y_final(0)
    y_final(1)
    w_final(0)
    w_final(1)
    y_final(2)
    w_final(2)
    y_final(3)
    y_drain()


def hand_over(a, b, c, d, oa, ob, oc, od, sem):
    copies = [
        pltpu.make_async_copy(src, dst, sem.at[n])
        for n, (src, dst) in enumerate(((b, ob), (c, oc), (d, od)))
    ]
    step = a.shape[0] // 4
    for n in range(4):
        rows = pl.ds(n * step, step)
        copies.append(pltpu.make_async_copy(a.at[rows, :], oa.at[rows, :], sem.at[3 + n]))
    for copy in copies:
        copy.start()
    for copy in copies:
        copy.wait()


def build(mesh, interpret_dims=None):
    chunk, dh = interpret_dims or (CHUNK, DH)

    def local(frames, grad_out, w_query, w_key, w_value):
        T, D = frames.shape
        G = w_query.shape[1]
        NM, NY = mesh.shape["tm"], mesh.shape["head"]
        NZ = NM // (NX * NC)
        NH = G // dh
        C = chunk
        NCH = T // C
        R, DB = D // NM, D // NY
        HB = DB // 2
        dims = dict(T=T, D=D, G=G, C=C, NZ=NZ, NY=NY, NH=NH, DH=dh)
        V = pltpu.VMEM
        S = pltpu.SemaphoreType.DMA
        scratch = [
            V((T, D), BF), V((T, G), BF), V((D, 3 * G), BF),
            V((T, G), BF), V((T, G), BF), V((T, G), BF),
            V((G, T), BF), V((G, T), BF), V((G, T), BF), V((D, T), BF),
            V((NCH, G, G), F32), V((NCH, G, G), F32),
            V((2, dh, G), F32), V((2, dh, G), BF),
            V((dh, G), BF), V((dh, G), F32), V((2, dh // 2, G), BF),
            V((2, NZ - 1, dh // 2, G), BF), V((dh, G), F32),
            V((3, dh // 2, G), BF), V((2, NX - 1, dh // 2, G), BF), V((dh, G), BF), V((dh, G), BF),
            V((2, dh, G), F32),
            V((3 * G, T), F32), V((3 * G, T), BF),
            V((NCH, NY, 2, HB, C), BF), V((NCH, 2, HB, C), BF), V((NCH, 2, 2, HB, C), BF),
            V((T, DB), BF), V((3, R, G), F32),
            V((3, NZ, NX, NC, R, G), BF), V((3, NZ, NX, R, G), BF),
            V((3, NX, 2, NZ // 2, R, G), BF), V((3, 2, NZ // 2, R, G), BF),
            V((3, 2, 2, NZ // 2, R, G), BF),
            V((3, NZ, R, G), BF), V((3, NZ, R, G), F32), V((3, NZ - 1, R, G), BF),
            S((4 + NCH,)), S((1,)), S((4,)), S((2,)), S((2, NZ - 1)), S((2,)),
            S((1,)), S((NCH, 2)), S((3,)), S((3,)), S((3, 2)), S((3,)),
        ]
        anyspace = pl.BlockSpec(memory_space=pl.ANY)
        hbm = pl.BlockSpec(memory_space=pltpu.HBM)
        shapes = [
            jax.ShapeDtypeStruct((T, DB), BF),
            jax.ShapeDtypeStruct((R, G), F32),
            jax.ShapeDtypeStruct((R, G), F32),
            jax.ShapeDtypeStruct((R, G), F32),
        ]
        results = pl.pallas_call(
            functools.partial(kernel, dims),
            out_shape=shapes,
            in_specs=[hbm] * 5,
            out_specs=[anyspace] * 4,
            scratch_shapes=scratch,
            compiler_params=pltpu.CompilerParams(
                collective_id=0, has_side_effects=True, vmem_limit_bytes=48 * 2**20
            ),
        )(
            *[
                pltpu.with_memory_space_constraint(array, pltpu.HBM)
                for array in (frames, grad_out, w_query, w_key, w_value)
            ]
        )
        return pl.pallas_call(
            hand_over,
            out_shape=shapes,
            in_specs=[anyspace] * 4,
            out_specs=[hbm] * 4,
            scratch_shapes=[S((7,))],
            compiler_params=pltpu.CompilerParams(vmem_limit_bytes=4 * 2**20),
        )(*results)

    placed = (P("tm", None), P("tm", "head"), P(None, "head"), P(None, "head"), P(None, "head"))
    return jax.shard_map(
        local,
        mesh=mesh,
        in_specs=placed,
        out_specs=(P("tm", "head"), P("tm", "head"), P("tm", "head"), P("tm", "head")),
        check_vma=False,
    )


def solution(mesh):
    return build(mesh)
```
